768 devices in a mesh: space: 96 (over x, z, core), group: 8 (over y).
Axes of the slice: x: 4, y: 8, z: 12, core: 2. Of those that a mesh axis runs over, the one named last changes fastest.
Arguments:
- point_feats: bfloat16 [1572864, 32], P(('space', 'group')), may hold values from -6 to 6
- point_voxel: int32 [1572864], P(('space', 'group')), may hold values from -1 to 4095, as said below
- cotangent: bfloat16 [1572864, 32], P(('space', 'group')), may hold values from -6 to 6
- kernel: bfloat16 [3, 3, 3, 32, 32], replicated, may hold values from -0.21875 to 0.21875
Outputs:
- point_grad: bfloat16 [1572864, 32], P(('space', 'group'))
The draws below stay inside these ranges and needn't reach their ends.
Inputs may be any that keep to these rules, and one draw needn't show every extreme that they name: `point_voxel`: in each block of 256 slots that one device sends to one member of its group the live slots come first and hold voxel numbers below 4096, the rest -1; every device fills one of its blocks completely.
All inputs are finite; a program needn't handle non-finite values.
Results may differ from the reference program's by a relative error of at most 0.0049.
Values may be sent and summed in bfloat16 or wider, within the bound.
No kernel may reach another device: no remote copies, remote signals or barrier semaphores. Data moves between devices by JAX's collectives and lax.ppermute only.
A program may use at most 64 MiB of HBM per device.

```python
import jax
import jax.numpy as jnp
from jax import lax

C = 32
XD = 16
YD = 16
ZB = 16
CAP = 256
V_DEV = 4096
NX = 1536
NY = 128
NPTS = 1572864
N_GROUP = 8


def draw_point_voxel(key, part):
    key_live, key_full, key_vox = jax.random.split(key, 3)
    blocks = NPTS // CAP
    live = jax.random.randint(key_live, (blocks,), 1, CAP + 1)
    senders = blocks // N_GROUP
    full = jax.random.randint(key_full, (senders,), 0, N_GROUP)
    number = jnp.arange(blocks)
    live = jnp.where(number % N_GROUP == full[number // N_GROUP], CAP, live)
    voxels = jax.random.randint(key_vox, (blocks, CAP), 0, V_DEV)
    slot = jnp.arange(CAP)[None, :]
    return jnp.where(slot < live[:, None], voxels, -1).reshape(NPTS).astype(jnp.int32)


def shard_levels(key, dims, shards, smallest, largest):
    def one(position, shards_of):
        heights = jax.random.uniform(jax.random.fold_in(jax.random.fold_in(key, 6), position), (shards_of,), jnp.float32, smallest / len(shards), largest / len(shards))
        return jnp.repeat(jnp.exp(heights), dims[position] // shards_of).reshape((-1,) + (1,) * (len(dims) - position - 1))

    factor_of = one(*shards[0])
    for cut in shards[1:]:
        factor_of = factor_of * one(*cut)
    return factor_of


def gaussian(key, shape, spread, bound, cuts=(), held_as=jnp.bfloat16):
    factor_of = shard_levels(key, shape, cuts, -0.22, 0.18) if cuts else 1.0
    result = jax.random.normal(key, shape, jnp.float32) * spread * factor_of
    return jnp.minimum(jnp.maximum(result, -bound), bound).astype(held_as)


def setup_inputs(seed: int = 0) -> dict:
    splits = jax.random.split(jax.random.key(seed), 5)
    point_feats = gaussian(splits[0], (NPTS, C), 1.0, 6.0, ((0, 768),))
    point_voxel = draw_point_voxel(jax.random.fold_in(splits[4], 71), 0)
    cotangent = gaussian(splits[2], (NPTS, C), 1.0, 6.0, ((0, 768),))
    kernel = gaussian(splits[3], (3, 3, 3, C, C), (27 * C) ** -0.5, 0.21875)
    return {"point_feats": point_feats, "point_voxel": point_voxel, "cotangent": cotangent, "kernel": kernel}


def convolve(padded, weights):
    return lax.conv_general_dilated(padded[None], weights, (1, 1, 1), "VALID", dimension_numbers=("NDHWC", "DHWIO", "NDHWC"), preferred_element_type=jnp.float32)[0]


def reference(point_feats, point_voxel, cotangent, kernel):
    rows = point_voxel.shape[0]
    order = jnp.arange(rows, dtype=jnp.int32)
    device = order // (N_GROUP * CAP)
    sx = device // N_GROUP
    block = (order % (N_GROUP * CAP)) // CAP
    live = point_voxel >= 0
    safe = jnp.where(live, point_voxel, 0)
    xl = safe // (YD * ZB)
    yl = (safe // ZB) % YD
    zl = safe % ZB
    total = NX * NY * ZB
    flat = ((sx * XD + xl) * NY + block * YD + yl) * ZB + zl
    flat = jnp.where(live, flat, total).astype(jnp.int32)
    sums = jax.ops.segment_sum(point_feats.astype(jnp.float32), flat, total + 1)
    counts = jax.ops.segment_sum(jnp.ones((rows,), jnp.float32), flat, total + 1)
    divisor = jnp.maximum(counts, 1.0)
    mean = (sums / divisor[:, None])[:total].reshape(NX, NY, ZB, C).astype(jnp.bfloat16)
    out = convolve(jnp.pad(mean, ((1, 1), (1, 1), (1, 1), (0, 0))), kernel)
    gy = jax.ops.segment_sum(cotangent.astype(jnp.float32), flat, total + 1)[:total].reshape(NX, NY, ZB, C)
    sig = jax.nn.sigmoid(out)
    gout = (gy * sig * (1.0 + out * (1.0 - sig))).astype(jnp.bfloat16)
    flipped = jnp.swapaxes(kernel[::-1, ::-1, ::-1], 3, 4)
    ggrid = convolve(jnp.pad(gout, ((1, 1), (1, 1), (1, 1), (0, 0))), flipped)
    table = jnp.concatenate([ggrid.reshape(total, C), jnp.zeros((1, C), jnp.float32)], axis=0)
    return (table[flat] / divisor[flat][:, None]).astype(jnp.bfloat16)
```

```python
import functools

import jax
import jax.numpy as jnp
from jax import lax
from jax.experimental import pallas as pl
from jax.experimental.pallas import tpu as pltpu
from jax.sharding import PartitionSpec as P

XD = 16
YD = 16
ZB = 16
C = 32
V_DEV = XD * YD * ZB
HALF = 64
PW = 2 * C + 3
TV = 512
TK = 512
TP = 256
TC = 512


def extended(shard, sides, width):
    for axis, dim in sides:
        size, length = (lax.axis_size(axis), shard.shape[dim])
        up = [(i, (i + 1) % size) for i in range(size - 1)]
        down = [(j, i) for i, j in up]
        last = lax.slice_in_dim(shard, length - width, length, axis=dim)
        first = lax.slice_in_dim(shard, 0, width, axis=dim)
        before = lax.ppermute(last, axis, up)
        after = lax.ppermute(first, axis, down)
        shard = jnp.concatenate([before, shard, after], axis=dim)
    return shard


def convolve(padded, weights):
    return lax.conv_general_dilated(
        padded[None],
        weights,
        (1, 1, 1),
        "VALID",
        dimension_numbers=("NDHWC", "DHWIO", "NDHWC"),
        preferred_element_type=jnp.float32,
    )[0]


def pad_depth(field):
    return jnp.pad(field, ((0, 0), (0, 0), (1, 1), (0, 0)))


def scatter_kernel(idx_ref, p_ref, out_ref):
    base = pl.program_id(0) * TV
    npts = p_ref.shape[0]
    acc = jnp.zeros((TV, PW), jnp.float32)
    rows = lax.broadcasted_iota(jnp.int32, (TV, TK), 0) + base
    for k in range(npts // TK):
        ids = idx_ref[:, pl.ds(k * TK, TK)]
        hot = (rows == ids).astype(jnp.bfloat16)
        acc = acc + jnp.dot(hot, p_ref[pl.ds(k * TK, TK), :], preferred_element_type=jnp.float32)
    col = lax.broadcasted_iota(jnp.int32, (TV, PW), 1)
    div = jnp.maximum(acc[:, 2 * C : 2 * C + 1], 1.0)
    mean = (acc / div).astype(jnp.bfloat16).astype(jnp.float32)
    out_ref[...] = jnp.where(col < C, mean, jnp.where(col == 2 * C, div, acc))


def scatter_sums(idx_row, payload):
    npts = payload.shape[0]
    return pl.pallas_call(
        scatter_kernel,
        out_shape=jax.ShapeDtypeStruct((V_DEV, PW), jnp.float32),
        grid=(V_DEV // TV,),
        in_specs=[
            pl.BlockSpec((1, npts), lambda t: (0, 0)),
            pl.BlockSpec((npts, PW), lambda t: (0, 0)),
        ],
        out_specs=pl.BlockSpec((TV, PW), lambda t: (t, 0)),
        cost_estimate=pl.CostEstimate(
            flops=2 * V_DEV * npts * 128, transcendentals=0, bytes_accessed=npts * PW * 2 + V_DEV * PW * 4
        ),
    )(idx_row, payload)


def gather_kernel(idx_ref, t_ref, o_ref):
    ids = idx_ref[...]
    acc = jnp.zeros((TP, C), jnp.float32)
    cols = lax.broadcasted_iota(jnp.int32, (TP, TC), 1)
    for c in range(V_DEV // TC):
        hot = (cols + c * TC == ids).astype(jnp.bfloat16)
        acc = acc + jnp.dot(hot, t_ref[pl.ds(c * TC, TC), :], preferred_element_type=jnp.float32)
    o_ref[...] = acc.astype(o_ref.dtype)


def gather_rows(idx_col, table):
    npts = idx_col.shape[0]
    return pl.pallas_call(
        gather_kernel,
        out_shape=jax.ShapeDtypeStruct((npts, C), jnp.bfloat16),
        grid=(npts // TP,),
        in_specs=[
            pl.BlockSpec((TP, 1), lambda t: (t, 0)),
            pl.BlockSpec((V_DEV, C), lambda t: (0, 0)),
        ],
        out_specs=pl.BlockSpec((TP, C), lambda t: (t, 0)),
        cost_estimate=pl.CostEstimate(
            flops=2 * V_DEV * npts * 128, transcendentals=0, bytes_accessed=npts * C * 2 + V_DEV * C * 2
        ),
    )(idx_col, table)


def per_device(point_feats, point_voxel, cotangent, kernel):
    npts = point_feats.shape[0]
    live = point_voxel >= 0
    hi = jnp.where(live, point_voxel // HALF, -1).astype(jnp.bfloat16)
    lo = jnp.where(live, point_voxel % HALF, 0).astype(jnp.bfloat16)
    payload = jnp.concatenate(
        [point_feats, cotangent, jnp.ones((npts, 1), jnp.bfloat16), hi[:, None], lo[:, None]], axis=1
    )
    got = lax.all_to_all(payload, "group", split_axis=0, concat_axis=0, tiled=True)
    index = got[:, 2 * C + 1].astype(jnp.int32) * HALF + got[:, 2 * C + 2].astype(jnp.int32)
    stats = scatter_sums(index.reshape(1, npts), got)
    divisor = stats[:, 2 * C]
    field = stats[:, : 2 * C].reshape(XD, YD, ZB, 2 * C)
    wide = extended(field, (("space", 0), ("group", 1)), 2)
    mean = wide[..., :C].astype(jnp.bfloat16)
    out = convolve(pad_depth(mean), kernel)
    gy = wide[1:-1, 1:-1, :, C:]
    sig = jax.nn.sigmoid(out)
    gout = (gy * sig * (1.0 + out * (1.0 - sig))).astype(jnp.bfloat16)
    flipped = jnp.swapaxes(kernel[::-1, ::-1, ::-1], 3, 4)
    ggrid = convolve(pad_depth(gout), flipped)
    table = (ggrid.reshape(V_DEV, C) / divisor[:, None]).astype(jnp.bfloat16)
    grads = gather_rows(index.reshape(npts, 1), table)
    return lax.all_to_all(grads, "group", split_axis=0, concat_axis=0, tiled=True)


def solution(mesh):
    placed = (P(("space", "group"), None), P(("space", "group")), P(("space", "group"), None), P())
    return jax.shard_map(
        per_device,
        mesh=mesh,
        in_specs=placed,
        out_specs=P(("space", "group"), None),
        check_vma=False,
    )
```

```python
import jax
import jax.numpy as jnp
from jax import lax
from jax.experimental import pallas as pl
from jax.experimental.pallas import tpu as pltpu
from jax.sharding import PartitionSpec as P

XD = 16
YD = 16
ZB = 16
C = 32
XY = XD * YD
ZC = ZB * C
HALF = 64
PW = 2 * C + 2
TK = 512
EX = XD + 4
EY = YD + 4
ER = EX * EY


def extended(shard, sides, width):
    for axis, dim in sides:
        size, length = (lax.axis_size(axis), shard.shape[dim])
        up = [(i, (i + 1) % size) for i in range(size - 1)]
        down = [(j, i) for i, j in up]
        last = lax.slice_in_dim(shard, length - width, length, axis=dim)
        first = lax.slice_in_dim(shard, 0, width, axis=dim)
        before = lax.ppermute(last, axis, up)
        after = lax.ppermute(first, axis, down)
        shard = jnp.concatenate([before, shard, after], axis=dim)
    return shard


def scatter_kernel(got_ref, xy_ref, z_ref, mean_ref, gy_ref, div_ref):
    npts = got_ref.shape[0]
    r = lax.broadcasted_iota(jnp.int32, (PW, ZC), 0)
    l = lax.broadcasted_iota(jnp.int32, (PW, ZC), 1)
    ef = (r == jnp.bitwise_and(l, C - 1)).astype(jnp.bfloat16)
    ec = (r == jnp.bitwise_and(l, C - 1) + C).astype(jnp.bfloat16)
    lane_z = lax.broadcasted_iota(jnp.int32, (TK, ZC), 1) >> 5
    rows = lax.broadcasted_iota(jnp.int32, (XY, TK), 0)
    sf = jnp.zeros((XY, ZC), jnp.float32)
    sc = jnp.zeros((XY, ZC), jnp.float32)
    sn = jnp.zeros((XY, ZC), jnp.float32)
    for k in range(npts // TK):
        g = got_ref[pl.ds(k * TK, TK), :]
        mask = lane_z == z_ref[pl.ds(k * TK, TK), :]
        tf = jnp.dot(g, ef, preferred_element_type=jnp.float32)
        tc = jnp.dot(g, ec, preferred_element_type=jnp.float32)
        qf = jnp.where(mask, tf, 0.0).astype(jnp.bfloat16)
        qc = jnp.where(mask, tc, 0.0).astype(jnp.bfloat16)
        qn = mask.astype(jnp.bfloat16)
        hot = (rows == xy_ref[:, pl.ds(k * TK, TK)]).astype(jnp.bfloat16)
        sf = sf + jnp.dot(hot, qf, preferred_element_type=jnp.float32)
        sc = sc + jnp.dot(hot, qc, preferred_element_type=jnp.float32)
        sn = sn + jnp.dot(hot, qn, preferred_element_type=jnp.float32)
    div = jnp.maximum(sn, 1.0)
    mean_ref[...] = (sf / div).astype(jnp.bfloat16).astype(jnp.float32)
    gy_ref[...] = sc
    div_ref[...] = div


def scatter_sums(got, xy_row, z_col):
    npts = got.shape[0]
    field = jax.ShapeDtypeStruct((XY, ZC), jnp.float32)
    return pl.pallas_call(
        scatter_kernel,
        out_shape=(field, field, field),
        cost_estimate=pl.CostEstimate(
            flops=2 * XY * npts * ZC * 3 + 4 * npts * PW * ZC, transcendentals=0,
            bytes_accessed=npts * PW * 2 + 3 * XY * ZC * 4,
        ),
    )(got, xy_row, z_col)


def conv_kernel(m_ref, g_ref, w_ref, o_ref):
    mean = m_ref[...]
    acc = jnp.zeros((ER, ZC), jnp.float32)
    for a in range(3):
        for b in range(3):
            off = (a - 1) * EY + (b - 1)
            part = jnp.dot(mean, w_ref[a * 3 + b], preferred_element_type=jnp.float32)
            acc = acc + pltpu.roll(part, (-off) % ER, 0)
    sig = 1.0 / (1.0 + jnp.exp(-acc))
    gout = (g_ref[...] * sig * (1.0 + acc * (1.0 - sig))).astype(jnp.bfloat16)
    acc = jnp.zeros((ER, ZC), jnp.float32)
    for a in range(3):
        for b in range(3):
            off = (a - 1) * EY + (b - 1)
            part = lax.dot_general(
                gout, w_ref[8 - (a * 3 + b)], (((1,), (1,)), ((), ())), preferred_element_type=jnp.float32
            )
            acc = acc + pltpu.roll(part, (-off) % ER, 0)
    o_ref[...] = acc


def conv_pair(mean_ext, gy_ext, banded):
    return pl.pallas_call(
        conv_kernel,
        out_shape=jax.ShapeDtypeStruct((ER, ZC), jnp.float32),
        compiler_params=pltpu.CompilerParams(vmem_limit_bytes=48 * 1024 * 1024),
        cost_estimate=pl.CostEstimate(
            flops=18 * 2 * ER * ZC * ZC, transcendentals=ER * ZC,
            bytes_accessed=ER * ZC * 10 + 9 * ZC * ZC * 2,
        ),
    )(mean_ext, gy_ext, banded)


def gather_kernel(t_ref, xy_ref, z_ref, o_ref):
    npts = o_ref.shape[0]
    r = lax.broadcasted_iota(jnp.int32, (ZC, C), 0)
    l = lax.broadcasted_iota(jnp.int32, (ZC, C), 1)
    fold = (jnp.bitwise_and(r, C - 1) == l).astype(jnp.bfloat16)
    lane_z = lax.broadcasted_iota(jnp.int32, (TK, ZC), 1) >> 5
    cols = lax.broadcasted_iota(jnp.int32, (TK, XY), 1)
    table = t_ref[...]
    for k in range(npts // TK):
        hot = (cols == xy_ref[pl.ds(k * TK, TK), :]).astype(jnp.bfloat16)
        rows = jnp.dot(hot, table, preferred_element_type=jnp.float32)
        mask = lane_z == z_ref[pl.ds(k * TK, TK), :]
        picked = jnp.where(mask, rows, 0.0).astype(jnp.bfloat16)
        o_ref[pl.ds(k * TK, TK), :] = jnp.dot(picked, fold, preferred_element_type=jnp.float32).astype(o_ref.dtype)


def gather_rows(table, xy_col, z_col):
    npts = xy_col.shape[0]
    return pl.pallas_call(
        gather_kernel,
        out_shape=jax.ShapeDtypeStruct((npts, C), jnp.bfloat16),
        cost_estimate=pl.CostEstimate(
            flops=2 * npts * XY * ZC + 2 * npts * ZC * C, transcendentals=0,
            bytes_accessed=npts * C * 2 + XY * ZC * 2,
        ),
    )(table, xy_col, z_col)


def banded_weights(kernel):
    zi = jnp.arange(ZB)
    shift = (zi[None, :, None] == zi[None, None, :] + jnp.arange(3)[:, None, None] - 1).astype(kernel.dtype)
    wide = jnp.einsum("dab,xydio->xyaibo", shift, kernel, preferred_element_type=jnp.float32)
    return wide.astype(kernel.dtype).reshape(9, ZC, ZC)


def per_device(point_feats, point_voxel, cotangent, kernel):
    npts = point_feats.shape[0]
    live = point_voxel >= 0
    hi = jnp.where(live, point_voxel // HALF, -1).astype(jnp.bfloat16)
    lo = jnp.where(live, point_voxel % HALF, 0).astype(jnp.bfloat16)
    payload = jnp.concatenate([point_feats, cotangent, hi[:, None], lo[:, None]], axis=1)
    got = lax.all_to_all(payload, "group", split_axis=0, concat_axis=0, tiled=True)
    index = got[:, 2 * C].astype(jnp.int32) * HALF + got[:, 2 * C + 1].astype(jnp.int32)
    xy = jnp.where(index >= 0, index >> 4, -1)
    z = jnp.bitwise_and(index, ZB - 1)
    mean, gy, divisor = scatter_sums(got, xy.reshape(1, npts), z.reshape(npts, 1))
    field = jnp.concatenate([mean, gy], axis=1).reshape(XD, YD, 2 * ZC)
    wide = extended(field, (("space", 0), ("group", 1)), 2)
    mean_ext = wide[..., :ZC].astype(jnp.bfloat16).reshape(ER, ZC)
    gy_ext = wide[..., ZC:].reshape(ER, ZC)
    ggrid = conv_pair(mean_ext, gy_ext, banded_weights(kernel))
    center = ggrid.reshape(EX, EY, ZC)[2 : 2 + XD, 2 : 2 + YD].reshape(XY, ZC)
    table = (center / divisor).astype(jnp.bfloat16)
    grads = gather_rows(table, xy.reshape(npts, 1), z.reshape(npts, 1))
    return lax.all_to_all(grads, "group", split_axis=0, concat_axis=0, tiled=True)


def solution(mesh):
    placed = (P(("space", "group"), None), P(("space", "group")), P(("space", "group"), None), P())
    return jax.shard_map(
        per_device,
        mesh=mesh,
        in_specs=placed,
        out_specs=P(("space", "group"), None),
        check_vma=False,
    )
```

```python
import jax
import jax.numpy as jnp
from jax import lax
from jax.experimental import pallas as pl
from jax.experimental.pallas import tpu as pltpu
from jax.sharding import PartitionSpec as P

XD = 16
YD = 16
ZB = 16
C = 32
XY = XD * YD
ZC = ZB * C
PW = 2 * C + 2
TK = 512
EX = XD + 4
EY = YD + 4
ER = EX * EY


def extended(shard, sides, width):
    for axis, dim in sides:
        size, length = (lax.axis_size(axis), shard.shape[dim])
        up = [(i, (i + 1) % size) for i in range(size - 1)]
        down = [(j, i) for i, j in up]
        last = lax.slice_in_dim(shard, length - width, length, axis=dim)
        first = lax.slice_in_dim(shard, 0, width, axis=dim)
        before = lax.ppermute(last, axis, up)
        after = lax.ppermute(first, axis, down)
        shard = jnp.concatenate([before, shard, after], axis=dim)
    return shard


def scatter_kernel(got_ref, xy_ref, z_ref, mean_ref, gy_ref, div_ref):
    npts = got_ref.shape[0]
    r = lax.broadcasted_iota(jnp.int32, (PW, ZC), 0)
    l = lax.broadcasted_iota(jnp.int32, (PW, ZC), 1)
    ef = (r == jnp.bitwise_and(l, C - 1)).astype(jnp.bfloat16)
    ec = (r == jnp.bitwise_and(l, C - 1) + C).astype(jnp.bfloat16)
    lane_z = lax.broadcasted_iota(jnp.int32, (TK, ZC), 1) >> 5
    rows = lax.broadcasted_iota(jnp.int32, (XY, TK), 0)
    sf = jnp.zeros((XY, ZC), jnp.float32)
    sc = jnp.zeros((XY, ZC), jnp.float32)
    sn = jnp.zeros((XY, ZC), jnp.float32)
    for k in range(npts // TK):
        g = got_ref[pl.ds(k * TK, TK), :]
        mask = lane_z == z_ref[pl.ds(k * TK, TK), :]
        tf = jnp.dot(g, ef, preferred_element_type=jnp.float32)
        tc = jnp.dot(g, ec, preferred_element_type=jnp.float32)
        qf = jnp.where(mask, tf, 0.0).astype(jnp.bfloat16)
        qc = jnp.where(mask, tc, 0.0).astype(jnp.bfloat16)
        qn = mask.astype(jnp.bfloat16)
        hot = (rows == xy_ref[:, pl.ds(k * TK, TK)]).astype(jnp.bfloat16)
        sf = sf + jnp.dot(hot, qf, preferred_element_type=jnp.float32)
        sc = sc + jnp.dot(hot, qc, preferred_element_type=jnp.float32)
        sn = sn + jnp.dot(hot, qn, preferred_element_type=jnp.float32)
    div = jnp.maximum(sn, 1.0)
    mean_ref[...] = (sf / div).astype(jnp.bfloat16).astype(jnp.float32)
    gy_ref[...] = sc
    div_ref[...] = div


def scatter_sums(got, xy_row, z_col):
    npts = got.shape[0]
    field = jax.ShapeDtypeStruct((XY, ZC), jnp.float32)
    return pl.pallas_call(
        scatter_kernel,
        out_shape=(field, field, field),
        cost_estimate=pl.CostEstimate(
            flops=2 * XY * npts * ZC * 3 + 4 * npts * PW * ZC, transcendentals=0,
            bytes_accessed=npts * PW * 2 + 3 * XY * ZC * 4,
        ),
    )(got, xy_row, z_col)


def conv_kernel(m_ref, g_ref, w_ref, o_ref):
    mean = m_ref[...]
    acc = jnp.zeros((ER, ZC), jnp.float32)
    for a in range(3):
        for b in range(3):
            off = (a - 1) * EY + (b - 1)
            part = jnp.dot(mean, w_ref[a * 3 + b], preferred_element_type=jnp.float32)
            acc = acc + pltpu.roll(part, (-off) % ER, 0)
    sig = 1.0 / (1.0 + jnp.exp(-acc))
    gout = (g_ref[...] * sig * (1.0 + acc * (1.0 - sig))).astype(jnp.bfloat16)
    acc = jnp.zeros((ER, ZC), jnp.float32)
    for a in range(3):
        for b in range(3):
            off = (a - 1) * EY + (b - 1)
            part = lax.dot_general(
                gout, w_ref[8 - (a * 3 + b)], (((1,), (1,)), ((), ())), preferred_element_type=jnp.float32
            )
            acc = acc + pltpu.roll(part, (-off) % ER, 0)
    o_ref[...] = acc


def conv_pair(mean_ext, gy_ext, banded):
    return pl.pallas_call(
        conv_kernel,
        out_shape=jax.ShapeDtypeStruct((ER, ZC), jnp.float32),
        compiler_params=pltpu.CompilerParams(vmem_limit_bytes=48 * 1024 * 1024),
        cost_estimate=pl.CostEstimate(
            flops=18 * 2 * ER * ZC * ZC, transcendentals=ER * ZC,
            bytes_accessed=ER * ZC * 10 + 9 * ZC * ZC * 2,
        ),
    )(mean_ext, gy_ext, banded)


def gather_kernel(t_ref, xy_ref, z_ref, o_ref):
    npts = o_ref.shape[0]
    r = lax.broadcasted_iota(jnp.int32, (ZC, C), 0)
    l = lax.broadcasted_iota(jnp.int32, (ZC, C), 1)
    fold = (jnp.bitwise_and(r, C - 1) == l).astype(jnp.bfloat16)
    lane_z = lax.broadcasted_iota(jnp.int32, (TK, ZC), 1) >> 5
    cols = lax.broadcasted_iota(jnp.int32, (TK, XY), 1)
    table = t_ref[...]
    for k in range(npts // TK):
        hot = (cols == xy_ref[pl.ds(k * TK, TK), :]).astype(jnp.bfloat16)
        rows = jnp.dot(hot, table, preferred_element_type=jnp.float32)
        mask = lane_z == z_ref[pl.ds(k * TK, TK), :]
        picked = jnp.where(mask, rows, 0.0).astype(jnp.bfloat16)
        o_ref[pl.ds(k * TK, TK), :] = jnp.dot(picked, fold, preferred_element_type=jnp.float32).astype(o_ref.dtype)


def gather_rows(table, xy_col, z_col):
    npts = xy_col.shape[0]
    return pl.pallas_call(
        gather_kernel,
        out_shape=jax.ShapeDtypeStruct((npts, C), jnp.bfloat16),
        cost_estimate=pl.CostEstimate(
            flops=2 * npts * XY * ZC + 2 * npts * ZC * C, transcendentals=0,
            bytes_accessed=npts * C * 2 + XY * ZC * 2,
        ),
    )(table, xy_col, z_col)


def band_kernel(w_ref, wb_ref):
    rr = lax.broadcasted_iota(jnp.int32, (ZC, C), 0)
    rc = lax.broadcasted_iota(jnp.int32, (ZC, C), 1)
    rep_rows = (jnp.bitwise_and(rr, C - 1) == rc).astype(jnp.bfloat16)
    lr = lax.broadcasted_iota(jnp.int32, (C, ZC), 0)
    lc = lax.broadcasted_iota(jnp.int32, (C, ZC), 1)
    rep_lanes = (lr == jnp.bitwise_and(lc, C - 1)).astype(jnp.bfloat16)
    diff = (lax.broadcasted_iota(jnp.int32, (ZC, ZC), 0) >> 5) - (lax.broadcasted_iota(jnp.int32, (ZC, ZC), 1) >> 5)
    acc = jnp.zeros((ZC, ZC), jnp.float32)
    for dz in range(3):
        wide = jnp.dot(w_ref[dz], rep_lanes, preferred_element_type=jnp.float32).astype(jnp.bfloat16)
        tiled = jnp.dot(rep_rows, wide, preferred_element_type=jnp.float32)
        acc = jnp.where(diff == dz - 1, tiled, acc)
    wb_ref[...] = acc.astype(wb_ref.dtype)


def banded_weights(kernel):
    taps = kernel.reshape(27, C, C)
    return pl.pallas_call(
        band_kernel,
        out_shape=jax.ShapeDtypeStruct((9, ZC, ZC), kernel.dtype),
        grid=(9,),
        in_specs=[pl.BlockSpec((3, C, C), lambda t: (t, 0, 0))],
        out_specs=pl.BlockSpec((None, ZC, ZC), lambda t: (t, 0, 0)),
        cost_estimate=pl.CostEstimate(
            flops=9 * 3 * 2 * 2 * ZC * C * ZC, transcendentals=0, bytes_accessed=9 * ZC * ZC * 2
        ),
    )(taps)


def per_device(point_feats, point_voxel, cotangent, kernel):
    npts = point_feats.shape[0]
    live = point_voxel >= 0
    xy_send = jnp.where(live, point_voxel >> 4, -1).astype(jnp.bfloat16)
    z_send = jnp.bitwise_and(point_voxel, ZB - 1).astype(jnp.bfloat16)
    payload = jnp.concatenate([point_feats, cotangent, xy_send[:, None], z_send[:, None]], axis=1)
    got = lax.all_to_all(payload, "group", split_axis=0, concat_axis=0, tiled=True)
    xy = got[:, 2 * C].astype(jnp.int32)
    z = got[:, 2 * C + 1].astype(jnp.int32)
    mean, gy, divisor = scatter_sums(got, xy.reshape(1, npts), z.reshape(npts, 1))
    field = jnp.concatenate([mean, gy], axis=1).reshape(XD, YD, 2 * ZC)
    wide = extended(field, (("space", 0), ("group", 1)), 2)
    mean_ext = wide[..., :ZC].astype(jnp.bfloat16).reshape(ER, ZC)
    gy_ext = wide[..., ZC:].reshape(ER, ZC)
    ggrid = conv_pair(mean_ext, gy_ext, banded_weights(kernel))
    center = ggrid.reshape(EX, EY, ZC)[2 : 2 + XD, 2 : 2 + YD].reshape(XY, ZC)
    table = (center / divisor).astype(jnp.bfloat16)
    grads = gather_rows(table, xy.reshape(npts, 1), z.reshape(npts, 1))
    return lax.all_to_all(grads, "group", split_axis=0, concat_axis=0, tiled=True)


def solution(mesh):
    placed = (P(("space", "group"), None), P(("space", "group")), P(("space", "group"), None), P())
    return jax.shard_map(
        per_device,
        mesh=mesh,
        in_specs=placed,
        out_specs=P(("space", "group"), None),
        check_vma=False,
    )
```

```python
import jax
import jax.numpy as jnp
from jax import lax
from jax.experimental import pallas as pl
from jax.experimental.pallas import tpu as pltpu
from jax.sharding import PartitionSpec as P

XD = 16
YD = 16
ZB = 16
C = 32
XY = XD * YD
ZC = ZB * C
PW = 2 * C + 2
TK = 512
EX = XD + 4
EY = YD + 4
ER = EX * EY


def extended(shard, sides, width):
    for axis, dim in sides:
        size, length = (lax.axis_size(axis), shard.shape[dim])
        up = [(i, (i + 1) % size) for i in range(size - 1)]
        down = [(j, i) for i, j in up]
        last = lax.slice_in_dim(shard, length - width, length, axis=dim)
        first = lax.slice_in_dim(shard, 0, width, axis=dim)
        before = lax.ppermute(last, axis, up)
        after = lax.ppermute(first, axis, down)
        shard = jnp.concatenate([before, shard, after], axis=dim)
    return shard


def scatter_kernel(got_ref, xy_ref, z_ref, mean_ref, gy_ref, div_ref):
    npts = got_ref.shape[0]
    r = lax.broadcasted_iota(jnp.int32, (PW, ZC), 0)
    l = lax.broadcasted_iota(jnp.int32, (PW, ZC), 1)
    ef = (r == jnp.bitwise_and(l, C - 1)).astype(jnp.bfloat16)
    ec = (r == jnp.bitwise_and(l, C - 1) + C).astype(jnp.bfloat16)
    lane_z = lax.broadcasted_iota(jnp.int32, (TK, ZC), 1) >> 5
    rows = lax.broadcasted_iota(jnp.int32, (XY, TK), 0)
    sf = jnp.zeros((XY, ZC), jnp.float32)
    sc = jnp.zeros((XY, ZC), jnp.float32)
    sn = jnp.zeros((XY, ZC), jnp.float32)
    for k in range(npts // TK):
        g = got_ref[pl.ds(k * TK, TK), :]
        mask = lane_z == z_ref[pl.ds(k * TK, TK), :]
        tf = jnp.dot(g, ef, preferred_element_type=jnp.float32)
        tc = jnp.dot(g, ec, preferred_element_type=jnp.float32)
        qf = jnp.where(mask, tf, 0.0).astype(jnp.bfloat16)
        qc = jnp.where(mask, tc, 0.0).astype(jnp.bfloat16)
        qn = mask.astype(jnp.bfloat16)
        hot = (rows == xy_ref[:, pl.ds(k * TK, TK)]).astype(jnp.bfloat16)
        sf = sf + jnp.dot(hot, qf, preferred_element_type=jnp.float32)
        sc = sc + jnp.dot(hot, qc, preferred_element_type=jnp.float32)
        sn = sn + jnp.dot(hot, qn, preferred_element_type=jnp.float32)
    div = jnp.maximum(sn, 1.0)
    mean_ref[...] = (sf / div).astype(jnp.bfloat16).astype(jnp.float32)
    gy_ref[...] = sc
    div_ref[...] = div


def scatter_sums(got, xy_row, z_col):
    npts = got.shape[0]
    field = jax.ShapeDtypeStruct((XY, ZC), jnp.float32)
    return pl.pallas_call(
        scatter_kernel,
        out_shape=(field, field, field),
        cost_estimate=pl.CostEstimate(
            flops=2 * XY * npts * ZC * 3 + 4 * npts * PW * ZC, transcendentals=0,
            bytes_accessed=npts * PW * 2 + 3 * XY * ZC * 4,
        ),
    )(got, xy_row, z_col)


def conv_kernel(m_ref, g_ref, w_ref, o_ref):
    mean = m_ref[...]
    acc = jnp.zeros((ER, ZC), jnp.float32)
    for a in range(3):
        for b in range(3):
            off = (a - 1) * EY + (b - 1)
            part = jnp.dot(mean, w_ref[a * 3 + b], preferred_element_type=jnp.float32)
            acc = acc + pltpu.roll(part, (-off) % ER, 0)
    sig = 1.0 / (1.0 + jnp.exp(-acc))
    gout = (g_ref[...] * sig * (1.0 + acc * (1.0 - sig))).astype(jnp.bfloat16)
    acc = jnp.zeros((ER, ZC), jnp.float32)
    for a in range(3):
        for b in range(3):
            off = (a - 1) * EY + (b - 1)
            part = lax.dot_general(
                gout, w_ref[8 - (a * 3 + b)], (((1,), (1,)), ((), ())), preferred_element_type=jnp.float32
            )
            acc = acc + pltpu.roll(part, (-off) % ER, 0)
    o_ref[...] = acc


def conv_pair(mean_ext, gy_ext, banded):
    return pl.pallas_call(
        conv_kernel,
        out_shape=jax.ShapeDtypeStruct((ER, ZC), jnp.float32),
        compiler_params=pltpu.CompilerParams(vmem_limit_bytes=48 * 1024 * 1024),
        cost_estimate=pl.CostEstimate(
            flops=18 * 2 * ER * ZC * ZC, transcendentals=ER * ZC,
            bytes_accessed=ER * ZC * 10 + 9 * ZC * ZC * 2,
        ),
    )(mean_ext, gy_ext, banded)


def gather_kernel(t_ref, xy_ref, z_ref, o_ref):
    npts = o_ref.shape[0]
    r = lax.broadcasted_iota(jnp.int32, (ZC, C), 0)
    l = lax.broadcasted_iota(jnp.int32, (ZC, C), 1)
    fold = (jnp.bitwise_and(r, C - 1) == l).astype(jnp.bfloat16)
    lane_z = lax.broadcasted_iota(jnp.int32, (TK, ZC), 1) >> 5
    cols = lax.broadcasted_iota(jnp.int32, (TK, XY), 1)
    table = t_ref[...]
    for k in range(npts // TK):
        hot = (cols == xy_ref[pl.ds(k * TK, TK), :]).astype(jnp.bfloat16)
        rows = jnp.dot(hot, table, preferred_element_type=jnp.float32)
        mask = lane_z == z_ref[pl.ds(k * TK, TK), :]
        picked = jnp.where(mask, rows, 0.0).astype(jnp.bfloat16)
        o_ref[pl.ds(k * TK, TK), :] = jnp.dot(picked, fold, preferred_element_type=jnp.float32).astype(o_ref.dtype)


def gather_rows(table, xy_col, z_col):
    npts = xy_col.shape[0]
    return pl.pallas_call(
        gather_kernel,
        out_shape=jax.ShapeDtypeStruct((npts, C), jnp.bfloat16),
        cost_estimate=pl.CostEstimate(
            flops=2 * npts * XY * ZC + 2 * npts * ZC * C, transcendentals=0,
            bytes_accessed=npts * C * 2 + XY * ZC * 2,
        ),
    )(table, xy_col, z_col)


def band_kernel(w_ref, wb_ref):
    lr = lax.broadcasted_iota(jnp.int32, (C, ZC), 0)
    lc = lax.broadcasted_iota(jnp.int32, (C, ZC), 1)
    rep_lanes = (lr == jnp.bitwise_and(lc, C - 1)).astype(jnp.bfloat16)
    lane_z = lc >> 5
    wides = [jnp.dot(w_ref[dz], rep_lanes, preferred_element_type=jnp.float32) for dz in range(3)]
    for zp in range(ZB):
        block = jnp.zeros((C, ZC), jnp.float32)
        for dz in range(3):
            block = jnp.where(lane_z == zp + 1 - dz, wides[dz], block)
        wb_ref[pl.ds(zp * C, C), :] = block.astype(wb_ref.dtype)


def banded_weights(kernel):
    taps = kernel.reshape(27, C, C)
    return pl.pallas_call(
        band_kernel,
        out_shape=jax.ShapeDtypeStruct((9, ZC, ZC), kernel.dtype),
        grid=(9,),
        in_specs=[pl.BlockSpec((3, C, C), lambda t: (t, 0, 0))],
        out_specs=pl.BlockSpec((None, ZC, ZC), lambda t: (t, 0, 0)),
        cost_estimate=pl.CostEstimate(
            flops=9 * 3 * 2 * 2 * ZC * C * ZC, transcendentals=0, bytes_accessed=9 * ZC * ZC * 2
        ),
    )(taps)


def per_device(point_feats, point_voxel, cotangent, kernel):
    npts = point_feats.shape[0]
    live = point_voxel >= 0
    xy_send = jnp.where(live, point_voxel >> 4, -1).astype(jnp.bfloat16)
    z_send = jnp.bitwise_and(point_voxel, ZB - 1).astype(jnp.bfloat16)
    payload = jnp.concatenate([point_feats, cotangent, xy_send[:, None], z_send[:, None]], axis=1)
    got = lax.all_to_all(payload, "group", split_axis=0, concat_axis=0, tiled=True)
    xy = got[:, 2 * C].astype(jnp.int32)
    z = got[:, 2 * C + 1].astype(jnp.int32)
    mean, gy, divisor = scatter_sums(got, xy.reshape(1, npts), z.reshape(npts, 1))
    field = jnp.concatenate([mean, gy], axis=1).reshape(XD, YD, 2 * ZC)
    wide = extended(field, (("space", 0), ("group", 1)), 2)
    mean_ext = wide[..., :ZC].astype(jnp.bfloat16).reshape(ER, ZC)
    gy_ext = wide[..., ZC:].reshape(ER, ZC)
    ggrid = conv_pair(mean_ext, gy_ext, banded_weights(kernel))
    center = ggrid.reshape(EX, EY, ZC)[2 : 2 + XD, 2 : 2 + YD].reshape(XY, ZC)
    table = (center / divisor).astype(jnp.bfloat16)
    grads = gather_rows(table, xy.reshape(npts, 1), z.reshape(npts, 1))
    return lax.all_to_all(grads, "group", split_axis=0, concat_axis=0, tiled=True)


def solution(mesh):
    placed = (P(("space", "group"), None), P(("space", "group")), P(("space", "group"), None), P())
    return jax.shard_map(
        per_device,
        mesh=mesh,
        in_specs=placed,
        out_specs=P(("space", "group"), None),
        check_vma=False,
    )
```

```python
import jax
import jax.numpy as jnp
from jax import lax
from jax.experimental import pallas as pl
from jax.experimental.pallas import tpu as pltpu
from jax.sharding import PartitionSpec as P

XD = 16
YD = 16
ZB = 16
C = 32
XY = XD * YD
ZC = ZB * C
PW = 2 * C + 2
TK = 512
EX = XD + 4
EY = YD + 4
ER = EX * EY


def extended(shard, sides, width):
    for axis, dim in sides:
        size, length = (lax.axis_size(axis), shard.shape[dim])
        up = [(i, (i + 1) % size) for i in range(size - 1)]
        down = [(j, i) for i, j in up]
        last = lax.slice_in_dim(shard, length - width, length, axis=dim)
        first = lax.slice_in_dim(shard, 0, width, axis=dim)
        before = lax.ppermute(last, axis, up)
        after = lax.ppermute(first, axis, down)
        shard = jnp.concatenate([before, shard, after], axis=dim)
    return shard


def scatter_kernel(got_ref, xy_ref, z_ref, field_ref, div_ref):
    npts = got_ref.shape[0]
    r = lax.broadcasted_iota(jnp.int32, (PW, ZC), 0)
    l = lax.broadcasted_iota(jnp.int32, (PW, ZC), 1)
    ef = (r == jnp.bitwise_and(l, C - 1)).astype(jnp.bfloat16)
    ec = (r == jnp.bitwise_and(l, C - 1) + C).astype(jnp.bfloat16)
    lane_z = lax.broadcasted_iota(jnp.int32, (TK, ZC), 1) >> 5
    rows = lax.broadcasted_iota(jnp.int32, (XY, TK), 0)
    sf = jnp.zeros((XY, ZC), jnp.float32)
    sc = jnp.zeros((XY, ZC), jnp.float32)
    sn = jnp.zeros((XY, ZC), jnp.float32)
    for k in range(npts // TK):
        g = got_ref[pl.ds(k * TK, TK), :]
        mask = lane_z == z_ref[pl.ds(k * TK, TK), :]
        tf = jnp.dot(g, ef, preferred_element_type=jnp.float32)
        tc = jnp.dot(g, ec, preferred_element_type=jnp.float32)
        qf = jnp.where(mask, tf, 0.0).astype(jnp.bfloat16)
        qc = jnp.where(mask, tc, 0.0).astype(jnp.bfloat16)
        qn = mask.astype(jnp.bfloat16)
        hot = (rows == xy_ref[:, pl.ds(k * TK, TK)]).astype(jnp.bfloat16)
        sf = sf + jnp.dot(hot, qf, preferred_element_type=jnp.float32)
        sc = sc + jnp.dot(hot, qc, preferred_element_type=jnp.float32)
        sn = sn + jnp.dot(hot, qn, preferred_element_type=jnp.float32)
    div = jnp.maximum(sn, 1.0)
    field_ref[:, :ZC] = (sf / div).astype(jnp.bfloat16).astype(jnp.float32)
    field_ref[:, ZC:] = sc
    div_ref[...] = div


def scatter_sums(got, xy_row, z_col):
    npts = got.shape[0]
    return pl.pallas_call(
        scatter_kernel,
        out_shape=(jax.ShapeDtypeStruct((XY, 2 * ZC), jnp.float32), jax.ShapeDtypeStruct((XY, ZC), jnp.float32)),
        cost_estimate=pl.CostEstimate(
            flops=2 * XY * npts * ZC * 3 + 4 * npts * PW * ZC, transcendentals=0,
            bytes_accessed=npts * PW * 2 + 3 * XY * ZC * 4,
        ),
    )(got, xy_row, z_col)


def conv_kernel(m_ref, g_ref, w_ref, o_ref):
    mean = m_ref[...]
    acc = jnp.zeros((ER, ZC), jnp.float32)
    for a in range(3):
        for b in range(3):
            off = (a - 1) * EY + (b - 1)
            part = jnp.dot(mean, w_ref[a * 3 + b], preferred_element_type=jnp.float32)
            acc = acc + pltpu.roll(part, (-off) % ER, 0)
    sig = 1.0 / (1.0 + jnp.exp(-acc))
    gout = (g_ref[...] * sig * (1.0 + acc * (1.0 - sig))).astype(jnp.bfloat16)
    acc = jnp.zeros((ER, ZC), jnp.float32)
    for a in range(3):
        for b in range(3):
            off = (a - 1) * EY + (b - 1)
            part = lax.dot_general(
                gout, w_ref[8 - (a * 3 + b)], (((1,), (1,)), ((), ())), preferred_element_type=jnp.float32
            )
            acc = acc + pltpu.roll(part, (-off) % ER, 0)
    o_ref[...] = acc


def conv_pair(mean_ext, gy_ext, banded):
    return pl.pallas_call(
        conv_kernel,
        out_shape=jax.ShapeDtypeStruct((ER, ZC), jnp.float32),
        compiler_params=pltpu.CompilerParams(vmem_limit_bytes=48 * 1024 * 1024),
        cost_estimate=pl.CostEstimate(
            flops=18 * 2 * ER * ZC * ZC, transcendentals=ER * ZC,
            bytes_accessed=ER * ZC * 10 + 9 * ZC * ZC * 2,
        ),
    )(mean_ext, gy_ext, banded)


def gather_kernel(t_ref, xy_ref, z_ref, o_ref):
    npts = o_ref.shape[0]
    r = lax.broadcasted_iota(jnp.int32, (ZC, C), 0)
    l = lax.broadcasted_iota(jnp.int32, (ZC, C), 1)
    fold = (jnp.bitwise_and(r, C - 1) == l).astype(jnp.bfloat16)
    lane_z = lax.broadcasted_iota(jnp.int32, (TK, ZC), 1) >> 5
    cols = lax.broadcasted_iota(jnp.int32, (TK, XY), 1)
    table = t_ref[...]
    for k in range(npts // TK):
        hot = (cols == xy_ref[pl.ds(k * TK, TK), :]).astype(jnp.bfloat16)
        rows = jnp.dot(hot, table, preferred_element_type=jnp.float32)
        mask = lane_z == z_ref[pl.ds(k * TK, TK), :]
        picked = jnp.where(mask, rows, 0.0).astype(jnp.bfloat16)
        o_ref[pl.ds(k * TK, TK), :] = jnp.dot(picked, fold, preferred_element_type=jnp.float32).astype(o_ref.dtype)


def gather_rows(table, xy_col, z_col):
    npts = xy_col.shape[0]
    return pl.pallas_call(
        gather_kernel,
        out_shape=jax.ShapeDtypeStruct((npts, C), jnp.bfloat16),
        cost_estimate=pl.CostEstimate(
            flops=2 * npts * XY * ZC + 2 * npts * ZC * C, transcendentals=0,
            bytes_accessed=npts * C * 2 + XY * ZC * 2,
        ),
    )(table, xy_col, z_col)


def band_kernel(w_ref, wb_ref):
    lr = lax.broadcasted_iota(jnp.int32, (C, ZC), 0)
    lc = lax.broadcasted_iota(jnp.int32, (C, ZC), 1)
    rep_lanes = (lr == jnp.bitwise_and(lc, C - 1)).astype(jnp.bfloat16)
    lane_z = (lc >> 5).astype(jnp.float32).astype(jnp.bfloat16)
    wides = [jnp.dot(w_ref[dz], rep_lanes, preferred_element_type=jnp.float32).astype(jnp.bfloat16) for dz in range(3)]
    zero = jnp.zeros((C, ZC), jnp.bfloat16)
    for zp in range(ZB):
        block = zero
        for dz in range(3):
            block = jnp.where(lane_z == jnp.bfloat16(zp + 1 - dz), wides[dz], block)
        wb_ref[pl.ds(zp * C, C), :] = block


def banded_weights(kernel):
    taps = kernel.reshape(27, C, C)
    return pl.pallas_call(
        band_kernel,
        out_shape=jax.ShapeDtypeStruct((9, ZC, ZC), kernel.dtype),
        grid=(9,),
        in_specs=[pl.BlockSpec((3, C, C), lambda t: (t, 0, 0))],
        out_specs=pl.BlockSpec((None, ZC, ZC), lambda t: (t, 0, 0)),
        cost_estimate=pl.CostEstimate(
            flops=9 * 3 * 2 * 2 * ZC * C * ZC, transcendentals=0, bytes_accessed=9 * ZC * ZC * 2
        ),
    )(taps)


def per_device(point_feats, point_voxel, cotangent, kernel):
    npts = point_feats.shape[0]
    live = point_voxel >= 0
    xy_send = jnp.where(live, point_voxel >> 4, -1).astype(jnp.bfloat16)
    z_send = jnp.bitwise_and(point_voxel, ZB - 1).astype(jnp.bfloat16)
    payload = jnp.concatenate([point_feats, cotangent, xy_send[:, None], z_send[:, None]], axis=1)
    got = lax.all_to_all(payload, "group", split_axis=0, concat_axis=0, tiled=True)
    xy = got[:, 2 * C].astype(jnp.int32)
    z = got[:, 2 * C + 1].astype(jnp.int32)
    field, divisor = scatter_sums(got, xy.reshape(1, npts), z.reshape(npts, 1))
    field = field.reshape(XD, YD, 2 * ZC)
    wide = extended(field, (("space", 0), ("group", 1)), 2)
    mean_ext = wide[..., :ZC].astype(jnp.bfloat16).reshape(ER, ZC)
    gy_ext = wide[..., ZC:].reshape(ER, ZC)
    ggrid = conv_pair(mean_ext, gy_ext, banded_weights(kernel))
    center = ggrid.reshape(EX, EY, ZC)[2 : 2 + XD, 2 : 2 + YD].reshape(XY, ZC)
    table = (center / divisor).astype(jnp.bfloat16)
    grads = gather_rows(table, xy.reshape(npts, 1), z.reshape(npts, 1))
    return lax.all_to_all(grads, "group", split_axis=0, concat_axis=0, tiled=True)


def solution(mesh):
    placed = (P(("space", "group"), None), P(("space", "group")), P(("space", "group"), None), P())
    return jax.shard_map(
        per_device,
        mesh=mesh,
        in_specs=placed,
        out_specs=P(("space", "group"), None),
        check_vma=False,
    )
```

```python
import jax
import jax.numpy as jnp
from jax import lax
from jax.experimental import pallas as pl
from jax.experimental.pallas import tpu as pltpu
from jax.sharding import PartitionSpec as P

XD = 16
YD = 16
ZB = 16
C = 32
XY = XD * YD
ZC = ZB * C
PW = 2 * C + 2
TK = 512
EX = XD + 4
EY = YD + 4
ER = EX * EY


def neighbour(block, shift_s, shift_g):
    ns, ng = lax.axis_size("space"), lax.axis_size("group")
    pairs = []
    for s in range(ns):
        for g in range(ng):
            t, h = s + shift_s, g + shift_g
            if 0 <= t < ns and 0 <= h < ng:
                pairs.append((s * ng + g, t * ng + h))
    return lax.ppermute(block, ("space", "group"), pairs)


def extended(field, width):
    lo, hi = slice(0, width), slice(field.shape[0] - width, field.shape[0])
    yl, yh = slice(0, width), slice(field.shape[1] - width, field.shape[1])
    x_before = neighbour(field[hi], 1, 0)
    x_after = neighbour(field[lo], -1, 0)
    y_before = neighbour(field[:, yh], 0, 1)
    y_after = neighbour(field[:, yl], 0, -1)
    c_mm = neighbour(field[hi, yh], 1, 1)
    c_mp = neighbour(field[hi, yl], 1, -1)
    c_pm = neighbour(field[lo, yh], -1, 1)
    c_pp = neighbour(field[lo, yl], -1, -1)
    top = jnp.concatenate([c_mm, x_before, c_mp], axis=1)
    mid = jnp.concatenate([y_before, field, y_after], axis=1)
    bot = jnp.concatenate([c_pm, x_after, c_pp], axis=1)
    return jnp.concatenate([top, mid, bot], axis=0)


def scatter_kernel(got_ref, xy_ref, z_ref, field_ref, div_ref):
    npts = got_ref.shape[0]
    r = lax.broadcasted_iota(jnp.int32, (PW, ZC), 0)
    l = lax.broadcasted_iota(jnp.int32, (PW, ZC), 1)
    ef = (r == jnp.bitwise_and(l, C - 1)).astype(jnp.bfloat16)
    ec = (r == jnp.bitwise_and(l, C - 1) + C).astype(jnp.bfloat16)
    lane_z = lax.broadcasted_iota(jnp.int32, (TK, ZC), 1) >> 5
    rows = lax.broadcasted_iota(jnp.int32, (XY, TK), 0)
    sf = jnp.zeros((XY, ZC), jnp.float32)
    sc = jnp.zeros((XY, ZC), jnp.float32)
    sn = jnp.zeros((XY, ZC), jnp.float32)
    for k in range(npts // TK):
        g = got_ref[pl.ds(k * TK, TK), :]
        mask = lane_z == z_ref[pl.ds(k * TK, TK), :]
        tf = jnp.dot(g, ef, preferred_element_type=jnp.float32)
        tc = jnp.dot(g, ec, preferred_element_type=jnp.float32)
        qf = jnp.where(mask, tf, 0.0).astype(jnp.bfloat16)
        qc = jnp.where(mask, tc, 0.0).astype(jnp.bfloat16)
        qn = mask.astype(jnp.bfloat16)
        hot = (rows == xy_ref[:, pl.ds(k * TK, TK)]).astype(jnp.bfloat16)
        sf = sf + jnp.dot(hot, qf, preferred_element_type=jnp.float32)
        sc = sc + jnp.dot(hot, qc, preferred_element_type=jnp.float32)
        sn = sn + jnp.dot(hot, qn, preferred_element_type=jnp.float32)
    div = jnp.maximum(sn, 1.0)
    field_ref[:, :ZC] = (sf / div).astype(jnp.bfloat16).astype(jnp.float32)
    field_ref[:, ZC:] = sc
    div_ref[...] = div


def scatter_sums(got, xy_row, z_col):
    npts = got.shape[0]
    return pl.pallas_call(
        scatter_kernel,
        out_shape=(jax.ShapeDtypeStruct((XY, 2 * ZC), jnp.float32), jax.ShapeDtypeStruct((XY, ZC), jnp.float32)),
        cost_estimate=pl.CostEstimate(
            flops=2 * XY * npts * ZC * 3 + 4 * npts * PW * ZC, transcendentals=0,
            bytes_accessed=npts * PW * 2 + 3 * XY * ZC * 4,
        ),
    )(got, xy_row, z_col)


def conv_kernel(m_ref, g_ref, w_ref, o_ref):
    mean = m_ref[...]
    acc = jnp.zeros((ER, ZC), jnp.float32)
    for a in range(3):
        for b in range(3):
            off = (a - 1) * EY + (b - 1)
            part = jnp.dot(mean, w_ref[a * 3 + b], preferred_element_type=jnp.float32)
            acc = acc + pltpu.roll(part, (-off) % ER, 0)
    sig = 1.0 / (1.0 + jnp.exp(-acc))
    gout = (g_ref[...] * sig * (1.0 + acc * (1.0 - sig))).astype(jnp.bfloat16)
    acc = jnp.zeros((ER, ZC), jnp.float32)
    for a in range(3):
        for b in range(3):
            off = (a - 1) * EY + (b - 1)
            part = lax.dot_general(
                gout, w_ref[8 - (a * 3 + b)], (((1,), (1,)), ((), ())), preferred_element_type=jnp.float32
            )
            acc = acc + pltpu.roll(part, (-off) % ER, 0)
    o_ref[...] = acc


def conv_pair(mean_ext, gy_ext, banded):
    return pl.pallas_call(
        conv_kernel,
        out_shape=jax.ShapeDtypeStruct((ER, ZC), jnp.float32),
        compiler_params=pltpu.CompilerParams(vmem_limit_bytes=48 * 1024 * 1024),
        cost_estimate=pl.CostEstimate(
            flops=18 * 2 * ER * ZC * ZC, transcendentals=ER * ZC,
            bytes_accessed=ER * ZC * 10 + 9 * ZC * ZC * 2,
        ),
    )(mean_ext, gy_ext, banded)


def gather_kernel(t_ref, xy_ref, z_ref, o_ref):
    npts = o_ref.shape[0]
    r = lax.broadcasted_iota(jnp.int32, (ZC, C), 0)
    l = lax.broadcasted_iota(jnp.int32, (ZC, C), 1)
    fold = (jnp.bitwise_and(r, C - 1) == l).astype(jnp.bfloat16)
    lane_z = lax.broadcasted_iota(jnp.int32, (TK, ZC), 1) >> 5
    cols = lax.broadcasted_iota(jnp.int32, (TK, XY), 1)
    table = t_ref[...]
    for k in range(npts // TK):
        hot = (cols == xy_ref[pl.ds(k * TK, TK), :]).astype(jnp.bfloat16)
        rows = jnp.dot(hot, table, preferred_element_type=jnp.float32)
        mask = lane_z == z_ref[pl.ds(k * TK, TK), :]
        picked = jnp.where(mask, rows, 0.0).astype(jnp.bfloat16)
        o_ref[pl.ds(k * TK, TK), :] = jnp.dot(picked, fold, preferred_element_type=jnp.float32).astype(o_ref.dtype)


def gather_rows(table, xy_col, z_col):
    npts = xy_col.shape[0]
    return pl.pallas_call(
        gather_kernel,
        out_shape=jax.ShapeDtypeStruct((npts, C), jnp.bfloat16),
        cost_estimate=pl.CostEstimate(
            flops=2 * npts * XY * ZC + 2 * npts * ZC * C, transcendentals=0,
            bytes_accessed=npts * C * 2 + XY * ZC * 2,
        ),
    )(table, xy_col, z_col)


def band_kernel(w_ref, wb_ref):
    lr = lax.broadcasted_iota(jnp.int32, (C, ZC), 0)
    lc = lax.broadcasted_iota(jnp.int32, (C, ZC), 1)
    rep_lanes = (lr == jnp.bitwise_and(lc, C - 1)).astype(jnp.bfloat16)
    lane_z = (lc >> 5).astype(jnp.float32).astype(jnp.bfloat16)
    wides = [jnp.dot(w_ref[dz], rep_lanes, preferred_element_type=jnp.float32).astype(jnp.bfloat16) for dz in range(3)]
    zero = jnp.zeros((C, ZC), jnp.bfloat16)
    for zp in range(ZB):
        block = zero
        for dz in range(3):
            block = jnp.where(lane_z == jnp.bfloat16(zp + 1 - dz), wides[dz], block)
        wb_ref[pl.ds(zp * C, C), :] = block


def banded_weights(kernel):
    taps = kernel.reshape(27, C, C)
    return pl.pallas_call(
        band_kernel,
        out_shape=jax.ShapeDtypeStruct((9, ZC, ZC), kernel.dtype),
        grid=(9,),
        in_specs=[pl.BlockSpec((3, C, C), lambda t: (t, 0, 0))],
        out_specs=pl.BlockSpec((None, ZC, ZC), lambda t: (t, 0, 0)),
        cost_estimate=pl.CostEstimate(
            flops=9 * 3 * 2 * 2 * ZC * C * ZC, transcendentals=0, bytes_accessed=9 * ZC * ZC * 2
        ),
    )(taps)


def per_device(point_feats, point_voxel, cotangent, kernel):
    npts = point_feats.shape[0]
    live = point_voxel >= 0
    xy_send = jnp.where(live, point_voxel >> 4, -1).astype(jnp.bfloat16)
    z_send = jnp.bitwise_and(point_voxel, ZB - 1).astype(jnp.bfloat16)
    payload = jnp.concatenate([point_feats, cotangent, xy_send[:, None], z_send[:, None]], axis=1)
    got = lax.all_to_all(payload, "group", split_axis=0, concat_axis=0, tiled=True)
    xy = got[:, 2 * C].astype(jnp.int32)
    z = got[:, 2 * C + 1].astype(jnp.int32)
    field, divisor = scatter_sums(got, xy.reshape(1, npts), z.reshape(npts, 1))
    field = field.reshape(XD, YD, 2 * ZC)
    wide = extended(field, 2)
    mean_ext = wide[..., :ZC].astype(jnp.bfloat16).reshape(ER, ZC)
    gy_ext = wide[..., ZC:].astype(jnp.float32).reshape(ER, ZC)
    ggrid = conv_pair(mean_ext, gy_ext, banded_weights(kernel))
    center = ggrid.reshape(EX, EY, ZC)[2 : 2 + XD, 2 : 2 + YD].reshape(XY, ZC)
    table = (center / divisor).astype(jnp.bfloat16)
    grads = gather_rows(table, xy.reshape(npts, 1), z.reshape(npts, 1))
    return lax.all_to_all(grads, "group", split_axis=0, concat_axis=0, tiled=True)


def solution(mesh):
    placed = (P(("space", "group"), None), P(("space", "group")), P(("space", "group"), None), P())
    return jax.shard_map(
        per_device,
        mesh=mesh,
        in_specs=placed,
        out_specs=P(("space", "group"), None),
        check_vma=False,
    )
```

```python
import jax
import jax.numpy as jnp
from jax import lax
from jax.experimental import pallas as pl
from jax.experimental.pallas import tpu as pltpu
from jax.sharding import PartitionSpec as P

XD = 16
YD = 16
ZB = 16
C = 32
XY = XD * YD
ZC = ZB * C
PW = 2 * C + 2
TK = 512
EX = XD + 4
EY = YD + 4
ER = EX * EY


def extended(shard, sides, width):
    for axis, dim in sides:
        size, length = (lax.axis_size(axis), shard.shape[dim])
        up = [(i, (i + 1) % size) for i in range(size - 1)]
        down = [(j, i) for i, j in up]
        last = lax.slice_in_dim(shard, length - width, length, axis=dim)
        first = lax.slice_in_dim(shard, 0, width, axis=dim)
        before = lax.ppermute(last, axis, up)
        after = lax.ppermute(first, axis, down)
        shard = jnp.concatenate([before, shard, after], axis=dim)
    return shard


def scatter_kernel(got_ref, field_ref, div_ref):
    npts = got_ref.shape[0]
    r = lax.broadcasted_iota(jnp.int32, (PW, ZC), 0)
    l = lax.broadcasted_iota(jnp.int32, (PW, ZC), 1)
    ef = (r == jnp.bitwise_and(l, C - 1)).astype(jnp.bfloat16)
    ec = (r == jnp.bitwise_and(l, C - 1) + C).astype(jnp.bfloat16)
    lane_z = (lax.broadcasted_iota(jnp.int32, (TK, ZC), 1) >> 5).astype(jnp.float32)
    lane_xy = lax.broadcasted_iota(jnp.int32, (TK, XY), 1).astype(jnp.float32)
    sf = jnp.zeros((XY, ZC), jnp.float32)
    sc = jnp.zeros((XY, ZC), jnp.float32)
    sn = jnp.zeros((XY, ZC), jnp.float32)
    over_points = (((0,), (0,)), ((), ()))
    for k in range(npts // TK):
        g = got_ref[pl.ds(k * TK, TK), :]
        wide = g.astype(jnp.float32)
        mask = lane_z == wide[:, 2 * C + 1 : 2 * C + 2]
        hot = (lane_xy == wide[:, 2 * C : 2 * C + 1]).astype(jnp.bfloat16)
        tf = jnp.dot(g, ef, preferred_element_type=jnp.float32)
        tc = jnp.dot(g, ec, preferred_element_type=jnp.float32)
        qf = jnp.where(mask, tf, 0.0).astype(jnp.bfloat16)
        qc = jnp.where(mask, tc, 0.0).astype(jnp.bfloat16)
        qn = mask.astype(jnp.bfloat16)
        sf = sf + lax.dot_general(hot, qf, over_points, preferred_element_type=jnp.float32)
        sc = sc + lax.dot_general(hot, qc, over_points, preferred_element_type=jnp.float32)
        sn = sn + lax.dot_general(hot, qn, over_points, preferred_element_type=jnp.float32)
    div = jnp.maximum(sn, 1.0)
    field_ref[:, :ZC] = (sf / div).astype(jnp.bfloat16).astype(jnp.float32)
    field_ref[:, ZC:] = sc
    div_ref[...] = div


def scatter_sums(got):
    npts = got.shape[0]
    return pl.pallas_call(
        scatter_kernel,
        out_shape=(jax.ShapeDtypeStruct((XY, 2 * ZC), jnp.float32), jax.ShapeDtypeStruct((XY, ZC), jnp.float32)),
        cost_estimate=pl.CostEstimate(
            flops=2 * XY * npts * ZC * 3 + 4 * npts * PW * ZC, transcendentals=0,
            bytes_accessed=npts * PW * 2 + 3 * XY * ZC * 4,
        ),
    )(got)


def conv_kernel(m_ref, g_ref, w_ref, o_ref):
    mean = m_ref[...]
    acc = jnp.zeros((ER, ZC), jnp.float32)
    for a in range(3):
        for b in range(3):
            off = (a - 1) * EY + (b - 1)
            part = jnp.dot(mean, w_ref[a * 3 + b], preferred_element_type=jnp.float32)
            acc = acc + pltpu.roll(part, (-off) % ER, 0)
    sig = 1.0 / (1.0 + jnp.exp(-acc))
    gout = (g_ref[...] * sig * (1.0 + acc * (1.0 - sig))).astype(jnp.bfloat16)
    acc = jnp.zeros((ER, ZC), jnp.float32)
    for a in range(3):
        for b in range(3):
            off = (a - 1) * EY + (b - 1)
            part = lax.dot_general(
                gout, w_ref[8 - (a * 3 + b)], (((1,), (1,)), ((), ())), preferred_element_type=jnp.float32
            )
            acc = acc + pltpu.roll(part, (-off) % ER, 0)
    o_ref[...] = acc


def conv_pair(mean_ext, gy_ext, banded):
    return pl.pallas_call(
        conv_kernel,
        out_shape=jax.ShapeDtypeStruct((ER, ZC), jnp.float32),
        compiler_params=pltpu.CompilerParams(vmem_limit_bytes=48 * 1024 * 1024),
        cost_estimate=pl.CostEstimate(
            flops=18 * 2 * ER * ZC * ZC, transcendentals=ER * ZC,
            bytes_accessed=ER * ZC * 10 + 9 * ZC * ZC * 2,
        ),
    )(mean_ext, gy_ext, banded)


def gather_kernel(t_ref, got_ref, o_ref):
    npts = o_ref.shape[0]
    r = lax.broadcasted_iota(jnp.int32, (ZC, C), 0)
    l = lax.broadcasted_iota(jnp.int32, (ZC, C), 1)
    fold = (jnp.bitwise_and(r, C - 1) == l).astype(jnp.bfloat16)
    lane_z = (lax.broadcasted_iota(jnp.int32, (TK, ZC), 1) >> 5).astype(jnp.float32)
    lane_xy = lax.broadcasted_iota(jnp.int32, (TK, XY), 1).astype(jnp.float32)
    table = t_ref[...]
    for k in range(npts // TK):
        wide = got_ref[pl.ds(k * TK, TK), :].astype(jnp.float32)
        hot = (lane_xy == wide[:, 2 * C : 2 * C + 1]).astype(jnp.bfloat16)
        rows = jnp.dot(hot, table, preferred_element_type=jnp.float32)
        mask = lane_z == wide[:, 2 * C + 1 : 2 * C + 2]
        picked = jnp.where(mask, rows, 0.0).astype(jnp.bfloat16)
        o_ref[pl.ds(k * TK, TK), :] = jnp.dot(picked, fold, preferred_element_type=jnp.float32).astype(o_ref.dtype)


def gather_rows(table, got):
    npts = got.shape[0]
    return pl.pallas_call(
        gather_kernel,
        out_shape=jax.ShapeDtypeStruct((npts, C), jnp.bfloat16),
        cost_estimate=pl.CostEstimate(
            flops=2 * npts * XY * ZC + 2 * npts * ZC * C, transcendentals=0,
            bytes_accessed=npts * C * 2 + XY * ZC * 2 + npts * PW * 2,
        ),
    )(table, got)


def band_kernel(w_ref, wb_ref):
    lr = lax.broadcasted_iota(jnp.int32, (C, ZC), 0)
    lc = lax.broadcasted_iota(jnp.int32, (C, ZC), 1)
    rep_lanes = (lr == jnp.bitwise_and(lc, C - 1)).astype(jnp.bfloat16)
    lane_z = (lc >> 5).astype(jnp.float32).astype(jnp.bfloat16)
    wides = [jnp.dot(w_ref[dz], rep_lanes, preferred_element_type=jnp.float32).astype(jnp.bfloat16) for dz in range(3)]
    zero = jnp.zeros((C, ZC), jnp.bfloat16)
    for zp in range(ZB):
        block = zero
        for dz in range(3):
            block = jnp.where(lane_z == jnp.bfloat16(zp + 1 - dz), wides[dz], block)
        wb_ref[pl.ds(zp * C, C), :] = block


def banded_weights(kernel):
    taps = kernel.reshape(27, C, C)
    return pl.pallas_call(
        band_kernel,
        out_shape=jax.ShapeDtypeStruct((9, ZC, ZC), kernel.dtype),
        grid=(9,),
        in_specs=[pl.BlockSpec((3, C, C), lambda t: (t, 0, 0))],
        out_specs=pl.BlockSpec((None, ZC, ZC), lambda t: (t, 0, 0)),
        cost_estimate=pl.CostEstimate(
            flops=9 * 3 * 2 * 2 * ZC * C * ZC, transcendentals=0, bytes_accessed=9 * ZC * ZC * 2
        ),
    )(taps)


def per_device(point_feats, point_voxel, cotangent, kernel):
    npts = point_feats.shape[0]
    live = point_voxel >= 0
    xy_send = jnp.where(live, point_voxel >> 4, -1).astype(jnp.bfloat16)
    z_send = jnp.bitwise_and(point_voxel, ZB - 1).astype(jnp.bfloat16)
    payload = jnp.concatenate([point_feats, cotangent, xy_send[:, None], z_send[:, None]], axis=1)
    got = lax.all_to_all(payload, "group", split_axis=0, concat_axis=0, tiled=True)
    field, divisor = scatter_sums(got)
    field = field.reshape(XD, YD, 2 * ZC)
    wide = extended(field, (("space", 0), ("group", 1)), 2)
    mean_ext = wide[..., :ZC].astype(jnp.bfloat16).reshape(ER, ZC)
    gy_ext = wide[..., ZC:].reshape(ER, ZC)
    ggrid = conv_pair(mean_ext, gy_ext, banded_weights(kernel))
    center = ggrid.reshape(EX, EY, ZC)[2 : 2 + XD, 2 : 2 + YD].reshape(XY, ZC)
    table = (center / divisor).astype(jnp.bfloat16)
    grads = gather_rows(table, got)
    return lax.all_to_all(grads, "group", split_axis=0, concat_axis=0, tiled=True)


def solution(mesh):
    placed = (P(("space", "group"), None), P(("space", "group")), P(("space", "group"), None), P())
    return jax.shard_map(
        per_device,
        mesh=mesh,
        in_specs=placed,
        out_specs=P(("space", "group"), None),
        check_vma=False,
    )
```

```python
import jax
import jax.numpy as jnp
from jax import lax
from jax.experimental import pallas as pl
from jax.experimental.pallas import tpu as pltpu
from jax.sharding import PartitionSpec as P

XD = 16
YD = 16
ZB = 16
C = 32
XY = XD * YD
ZC = ZB * C
PW = 2 * C + 2
TK = 512
EX = XD + 4
EY = YD + 4
ER = EX * EY


def extended(shard, sides, width):
    for axis, dim in sides:
        size, length = (lax.axis_size(axis), shard.shape[dim])
        up = [(i, (i + 1) % size) for i in range(size - 1)]
        down = [(j, i) for i, j in up]
        last = lax.slice_in_dim(shard, length - width, length, axis=dim)
        first = lax.slice_in_dim(shard, 0, width, axis=dim)
        before = lax.ppermute(last, axis, up)
        after = lax.ppermute(first, axis, down)
        shard = jnp.concatenate([before, shard, after], axis=dim)
    return shard


def scatter_kernel(got_ref, field_ref, div_ref):
    npts = got_ref.shape[0]
    r = lax.broadcasted_iota(jnp.int32, (PW, ZC), 0)
    l = lax.broadcasted_iota(jnp.int32, (PW, ZC), 1)
    ef = (r == jnp.bitwise_and(l, C - 1)).astype(jnp.bfloat16)
    ec = (r == jnp.bitwise_and(l, C - 1) + C).astype(jnp.bfloat16)
    lane_z = (lax.broadcasted_iota(jnp.int32, (TK, ZC), 1) >> 5).astype(jnp.float32)
    lane_xy = lax.broadcasted_iota(jnp.int32, (TK, XY), 1).astype(jnp.float32)
    sf = jnp.zeros((XY, ZC), jnp.float32)
    sc = jnp.zeros((XY, ZC), jnp.float32)
    sn = jnp.zeros((XY, ZC), jnp.float32)
    over_points = (((0,), (0,)), ((), ()))
    for k in range(npts // TK):
        g = got_ref[pl.ds(k * TK, TK), :]
        wide = g.astype(jnp.float32)
        mask = lane_z == wide[:, 2 * C + 1 : 2 * C + 2]
        hot = (lane_xy == wide[:, 2 * C : 2 * C + 1]).astype(jnp.bfloat16)
        tf = jnp.dot(g, ef, preferred_element_type=jnp.float32)
        tc = jnp.dot(g, ec, preferred_element_type=jnp.float32)
        qf = jnp.where(mask, tf, 0.0).astype(jnp.bfloat16)
        qc = jnp.where(mask, tc, 0.0).astype(jnp.bfloat16)
        qn = mask.astype(jnp.bfloat16)
        sf = sf + lax.dot_general(hot, qf, over_points, preferred_element_type=jnp.float32)
        sc = sc + lax.dot_general(hot, qc, over_points, preferred_element_type=jnp.float32)
        sn = sn + lax.dot_general(hot, qn, over_points, preferred_element_type=jnp.float32)
    div = jnp.maximum(sn, 1.0)
    field_ref[:, :ZC] = (sf / div).astype(jnp.bfloat16).astype(jnp.float32)
    field_ref[:, ZC:] = sc
    div_ref[...] = div


def scatter_sums(got):
    npts = got.shape[0]
    return pl.pallas_call(
        scatter_kernel,
        out_shape=(jax.ShapeDtypeStruct((XY, 2 * ZC), jnp.float32), jax.ShapeDtypeStruct((XY, ZC), jnp.float32)),
        cost_estimate=pl.CostEstimate(
            flops=2 * XY * npts * ZC * 3 + 4 * npts * PW * ZC, transcendentals=0,
            bytes_accessed=npts * PW * 2 + 3 * XY * ZC * 4,
        ),
    )(got)


def conv_kernel(m_ref, g_ref, w_ref, o_ref):
    mean = m_ref[...]
    acc = jnp.zeros((ER, ZC), jnp.float32)
    for a in range(3):
        for b in range(3):
            off = (a - 1) * EY + (b - 1)
            part = jnp.dot(mean, w_ref[a * 3 + b], preferred_element_type=jnp.float32)
            acc = acc + pltpu.roll(part, (-off) % ER, 0)
    sig = 1.0 / (1.0 + jnp.exp(-acc))
    gout = (g_ref[...] * sig * (1.0 + acc * (1.0 - sig))).astype(jnp.bfloat16)
    acc = jnp.zeros((ER, ZC), jnp.float32)
    for a in range(3):
        for b in range(3):
            off = (a - 1) * EY + (b - 1)
            part = lax.dot_general(
                gout, w_ref[8 - (a * 3 + b)], (((1,), (1,)), ((), ())), preferred_element_type=jnp.float32
            )
            acc = acc + pltpu.roll(part, (-off) % ER, 0)
    o_ref[...] = acc


def conv_pair(mean_ext, gy_ext, banded):
    return pl.pallas_call(
        conv_kernel,
        out_shape=jax.ShapeDtypeStruct((ER, ZC), jnp.float32),
        compiler_params=pltpu.CompilerParams(vmem_limit_bytes=48 * 1024 * 1024),
        cost_estimate=pl.CostEstimate(
            flops=18 * 2 * ER * ZC * ZC, transcendentals=ER * ZC,
            bytes_accessed=ER * ZC * 10 + 9 * ZC * ZC * 2,
        ),
    )(mean_ext, gy_ext, banded)


def gather_kernel(g_ref, d_ref, got_ref, o_ref, t_ref):
    npts = got_ref.shape[0]
    for x in range(XD):
        start = (x + 2) * EY + 2
        t_ref[pl.ds(x * YD, YD), :] = (g_ref[pl.ds(start, YD), :] / d_ref[pl.ds(x * YD, YD), :]).astype(t_ref.dtype)
    r = lax.broadcasted_iota(jnp.int32, (C, ZC), 0)
    l = lax.broadcasted_iota(jnp.int32, (C, ZC), 1)
    fold = (jnp.bitwise_and(l, C - 1) == r).astype(jnp.bfloat16)
    lane_z = (lax.broadcasted_iota(jnp.int32, (TK, ZC), 1) >> 5).astype(jnp.float32)
    lane_xy = lax.broadcasted_iota(jnp.int32, (TK, XY), 1).astype(jnp.float32)
    table = t_ref[...]
    block = o_ref.shape[2]
    for k in range(npts // TK):
        wide = got_ref[pl.ds(k * TK, TK), :].astype(jnp.float32)
        hot = (lane_xy == wide[:, 2 * C : 2 * C + 1]).astype(jnp.bfloat16)
        rows = jnp.dot(hot, table, preferred_element_type=jnp.float32)
        mask = lane_z == wide[:, 2 * C + 1 : 2 * C + 2]
        picked = jnp.where(mask, rows, 0.0).astype(jnp.bfloat16)
        out = lax.dot_general(fold, picked, (((1,), (1,)), ((), ())), preferred_element_type=jnp.float32)
        for j in range(TK // block):
            o_ref[k * (TK // block) + j] = out[:, j * block : (j + 1) * block].astype(o_ref.dtype)


def gather_rows(ggrid, divisor, got, parts):
    npts = got.shape[0]
    return pl.pallas_call(
        gather_kernel,
        out_shape=jax.ShapeDtypeStruct((parts, C, npts // parts), jnp.bfloat16),
        scratch_shapes=[pltpu.VMEM((XY, ZC), jnp.bfloat16)],
        cost_estimate=pl.CostEstimate(
            flops=2 * npts * XY * ZC + 2 * npts * ZC * C, transcendentals=0,
            bytes_accessed=npts * C * 2 + ER * ZC * 4 + XY * ZC * 4 + npts * PW * 2,
        ),
    )(ggrid, divisor, got)


def band_kernel(w_ref, wb_ref):
    lr = lax.broadcasted_iota(jnp.int32, (C, ZC), 0)
    lc = lax.broadcasted_iota(jnp.int32, (C, ZC), 1)
    rep_lanes = (lr == jnp.bitwise_and(lc, C - 1)).astype(jnp.bfloat16)
    lane_z = (lc >> 5).astype(jnp.float32).astype(jnp.bfloat16)
    wides = [jnp.dot(w_ref[dz], rep_lanes, preferred_element_type=jnp.float32).astype(jnp.bfloat16) for dz in range(3)]
    zero = jnp.zeros((C, ZC), jnp.bfloat16)
    for zp in range(ZB):
        block = zero
        for dz in range(3):
            block = jnp.where(lane_z == jnp.bfloat16(zp + 1 - dz), wides[dz], block)
        wb_ref[pl.ds(zp * C, C), :] = block


def banded_weights(kernel):
    taps = kernel.reshape(27, C, C)
    return pl.pallas_call(
        band_kernel,
        out_shape=jax.ShapeDtypeStruct((9, ZC, ZC), kernel.dtype),
        grid=(9,),
        in_specs=[pl.BlockSpec((3, C, C), lambda t: (t, 0, 0))],
        out_specs=pl.BlockSpec((None, ZC, ZC), lambda t: (t, 0, 0)),
        cost_estimate=pl.CostEstimate(
            flops=9 * 3 * 2 * 2 * ZC * C * ZC, transcendentals=0, bytes_accessed=9 * ZC * ZC * 2
        ),
    )(taps)


def per_device(point_feats, point_voxel, cotangent, kernel):
    npts = point_feats.shape[0]
    live = point_voxel >= 0
    xy_send = jnp.where(live, point_voxel >> 4, -1).astype(jnp.bfloat16)
    z_send = jnp.bitwise_and(point_voxel, ZB - 1).astype(jnp.bfloat16)
    payload = jnp.concatenate([point_feats, cotangent, xy_send[:, None], z_send[:, None]], axis=1)
    got = lax.all_to_all(payload, "group", split_axis=0, concat_axis=0, tiled=True)
    field, divisor = scatter_sums(got)
    field = field.reshape(XD, YD, 2 * ZC)
    wide = extended(field, (("space", 0), ("group", 1)), 2)
    mean_ext = wide[..., :ZC].astype(jnp.bfloat16).reshape(ER, ZC)
    gy_ext = wide[..., ZC:].reshape(ER, ZC)
    ggrid = conv_pair(mean_ext, gy_ext, banded_weights(kernel))
    parts = lax.axis_size("group")
    grads = gather_rows(ggrid, divisor, got, parts)
    back = lax.all_to_all(grads, "group", split_axis=0, concat_axis=0, tiled=True)
    return jnp.swapaxes(back, 1, 2).reshape(npts, C)


def solution(mesh):
    placed = (P(("space", "group"), None), P(("space", "group")), P(("space", "group"), None), P())
    return jax.shard_map(
        per_device,
        mesh=mesh,
        in_specs=placed,
        out_specs=P(("space", "group"), None),
        check_vma=False,
    )
```

```python
import jax
import jax.numpy as jnp
from jax import lax
from jax.experimental import pallas as pl
from jax.experimental.pallas import tpu as pltpu
from jax.sharding import PartitionSpec as P

XD = 16
YD = 16
ZB = 16
C = 32
XY = XD * YD
ZC = ZB * C
PW = 2 * C + 2
TK = 512
EX = XD + 4
EY = YD + 4
ER = EX * EY


def extended(shard, sides, width):
    for axis, dim in sides:
        size, length = (lax.axis_size(axis), shard.shape[dim])
        up = [(i, (i + 1) % size) for i in range(size - 1)]
        down = [(j, i) for i, j in up]
        last = lax.slice_in_dim(shard, length - width, length, axis=dim)
        first = lax.slice_in_dim(shard, 0, width, axis=dim)
        before = lax.ppermute(last, axis, up)
        after = lax.ppermute(first, axis, down)
        shard = jnp.concatenate([before, shard, after], axis=dim)
    return shard


def scatter_kernel(got_ref, field_ref, div_ref):
    npts = got_ref.shape[0]
    r = lax.broadcasted_iota(jnp.int32, (PW, ZC), 0)
    l = lax.broadcasted_iota(jnp.int32, (PW, ZC), 1)
    ef = (r == jnp.bitwise_and(l, C - 1)).astype(jnp.bfloat16)
    ec = (r == jnp.bitwise_and(l, C - 1) + C).astype(jnp.bfloat16)
    lane_z = (lax.broadcasted_iota(jnp.int32, (TK, ZC), 1) >> 5).astype(jnp.float32)
    lane_xy = lax.broadcasted_iota(jnp.int32, (TK, XY), 1).astype(jnp.float32)
    sf = jnp.zeros((XY, ZC), jnp.float32)
    sc = jnp.zeros((XY, ZC), jnp.float32)
    sn = jnp.zeros((XY, ZC), jnp.float32)
    over_points = (((0,), (0,)), ((), ()))
    for k in range(npts // TK):
        g = got_ref[pl.ds(k * TK, TK), :]
        wide = g.astype(jnp.float32)
        mask = lane_z == wide[:, 2 * C + 1 : 2 * C + 2]
        hot = (lane_xy == wide[:, 2 * C : 2 * C + 1]).astype(jnp.bfloat16)
        tf = jnp.dot(g, ef, preferred_element_type=jnp.float32)
        tc = jnp.dot(g, ec, preferred_element_type=jnp.float32)
        qf = jnp.where(mask, tf, 0.0).astype(jnp.bfloat16)
        qc = jnp.where(mask, tc, 0.0).astype(jnp.bfloat16)
        qn = mask.astype(jnp.bfloat16)
        sf = sf + lax.dot_general(hot, qf, over_points, preferred_element_type=jnp.float32)
        sc = sc + lax.dot_general(hot, qc, over_points, preferred_element_type=jnp.float32)
        sn = sn + lax.dot_general(hot, qn, over_points, preferred_element_type=jnp.float32)
    div = jnp.maximum(sn, 1.0)
    field_ref[:, :ZC] = (sf / div).astype(jnp.bfloat16).astype(jnp.float32)
    field_ref[:, ZC:] = sc
    div_ref[...] = div


def scatter_sums(got):
    npts = got.shape[0]
    return pl.pallas_call(
        scatter_kernel,
        out_shape=(jax.ShapeDtypeStruct((XY, 2 * ZC), jnp.float32), jax.ShapeDtypeStruct((XY, ZC), jnp.float32)),
        cost_estimate=pl.CostEstimate(
            flops=2 * XY * npts * ZC * 3 + 4 * npts * PW * ZC, transcendentals=0,
            bytes_accessed=npts * PW * 2 + 3 * XY * ZC * 4,
        ),
    )(got)


def conv_kernel(m_ref, g_ref, w_hbm, o_ref, w_ref, sems):
    copies = [pltpu.make_async_copy(w_hbm.at[t], w_ref.at[t], sems.at[t]) for t in range(9)]
    for cp in copies:
        cp.start()
    mean = m_ref[...]
    acc = jnp.zeros((ER, ZC), jnp.float32)
    for a in range(3):
        for b in range(3):
            off = (a - 1) * EY + (b - 1)
            copies[a * 3 + b].wait()
            part = jnp.dot(mean, w_ref[a * 3 + b], preferred_element_type=jnp.float32)
            acc = acc + pltpu.roll(part, (-off) % ER, 0)
    sig = 1.0 / (1.0 + jnp.exp(-acc))
    gout = (g_ref[...] * sig * (1.0 + acc * (1.0 - sig))).astype(jnp.bfloat16)
    acc = jnp.zeros((ER, ZC), jnp.float32)
    for a in range(3):
        for b in range(3):
            off = (a - 1) * EY + (b - 1)
            part = lax.dot_general(
                gout, w_ref[8 - (a * 3 + b)], (((1,), (1,)), ((), ())), preferred_element_type=jnp.float32
            )
            acc = acc + pltpu.roll(part, (-off) % ER, 0)
    o_ref[...] = acc


def conv_pair(mean_ext, gy_ext, banded):
    vmem = pl.BlockSpec(memory_space=pltpu.VMEM)
    return pl.pallas_call(
        conv_kernel,
        out_shape=jax.ShapeDtypeStruct((ER, ZC), jnp.float32),
        in_specs=[vmem, vmem, pl.BlockSpec(memory_space=pl.ANY)],
        out_specs=vmem,
        scratch_shapes=[pltpu.VMEM((9, ZC, ZC), jnp.bfloat16), pltpu.SemaphoreType.DMA((9,))],
        compiler_params=pltpu.CompilerParams(vmem_limit_bytes=48 * 1024 * 1024),
        cost_estimate=pl.CostEstimate(
            flops=18 * 2 * ER * ZC * ZC, transcendentals=ER * ZC,
            bytes_accessed=ER * ZC * 10 + 9 * ZC * ZC * 2,
        ),
    )(mean_ext, gy_ext, banded)


def gather_kernel(g_ref, d_ref, got_ref, o_ref, t_ref):
    npts = got_ref.shape[0]
    for x in range(XD):
        start = (x + 2) * EY + 2
        t_ref[pl.ds(x * YD, YD), :] = (g_ref[pl.ds(start, YD), :] / d_ref[pl.ds(x * YD, YD), :]).astype(t_ref.dtype)
    r = lax.broadcasted_iota(jnp.int32, (C, ZC), 0)
    l = lax.broadcasted_iota(jnp.int32, (C, ZC), 1)
    fold = (jnp.bitwise_and(l, C - 1) == r).astype(jnp.bfloat16)
    lane_z = (lax.broadcasted_iota(jnp.int32, (TK, ZC), 1) >> 5).astype(jnp.float32)
    lane_xy = lax.broadcasted_iota(jnp.int32, (TK, XY), 1).astype(jnp.float32)
    table = t_ref[...]
    block = o_ref.shape[2]
    for k in range(npts // TK):
        wide = got_ref[pl.ds(k * TK, TK), :].astype(jnp.float32)
        hot = (lane_xy == wide[:, 2 * C : 2 * C + 1]).astype(jnp.bfloat16)
        rows = jnp.dot(hot, table, preferred_element_type=jnp.float32)
        mask = lane_z == wide[:, 2 * C + 1 : 2 * C + 2]
        picked = jnp.where(mask, rows, 0.0).astype(jnp.bfloat16)
        out = lax.dot_general(fold, picked, (((1,), (1,)), ((), ())), preferred_element_type=jnp.float32)
        for j in range(TK // block):
            o_ref[k * (TK // block) + j] = out[:, j * block : (j + 1) * block].astype(o_ref.dtype)


def gather_rows(ggrid, divisor, got, parts):
    npts = got.shape[0]
    return pl.pallas_call(
        gather_kernel,
        out_shape=jax.ShapeDtypeStruct((parts, C, npts // parts), jnp.bfloat16),
        scratch_shapes=[pltpu.VMEM((XY, ZC), jnp.bfloat16)],
        cost_estimate=pl.CostEstimate(
            flops=2 * npts * XY * ZC + 2 * npts * ZC * C, transcendentals=0,
            bytes_accessed=npts * C * 2 + ER * ZC * 4 + XY * ZC * 4 + npts * PW * 2,
        ),
    )(ggrid, divisor, got)


def band_kernel(w_ref, wb_ref):
    lr = lax.broadcasted_iota(jnp.int32, (C, ZC), 0)
    lc = lax.broadcasted_iota(jnp.int32, (C, ZC), 1)
    rep_lanes = (lr == jnp.bitwise_and(lc, C - 1)).astype(jnp.bfloat16)
    lane_z = (lc >> 5).astype(jnp.float32).astype(jnp.bfloat16)
    wides = [jnp.dot(w_ref[dz], rep_lanes, preferred_element_type=jnp.float32).astype(jnp.bfloat16) for dz in range(3)]
    zero = jnp.zeros((C, ZC), jnp.bfloat16)
    for zp in range(ZB):
        block = zero
        for dz in range(3):
            block = jnp.where(lane_z == jnp.bfloat16(zp + 1 - dz), wides[dz], block)
        wb_ref[pl.ds(zp * C, C), :] = block


def banded_weights(kernel):
    taps = kernel.reshape(27, C, C)
    return pl.pallas_call(
        band_kernel,
        out_shape=jax.ShapeDtypeStruct((9, ZC, ZC), kernel.dtype),
        grid=(9,),
        in_specs=[pl.BlockSpec((3, C, C), lambda t: (t, 0, 0))],
        out_specs=pl.BlockSpec((None, ZC, ZC), lambda t: (t, 0, 0)),
        cost_estimate=pl.CostEstimate(
            flops=9 * 3 * 2 * 2 * ZC * C * ZC, transcendentals=0, bytes_accessed=9 * ZC * ZC * 2
        ),
    )(taps)


def per_device(point_feats, point_voxel, cotangent, kernel):
    npts = point_feats.shape[0]
    live = point_voxel >= 0
    xy_send = jnp.where(live, point_voxel >> 4, -1).astype(jnp.bfloat16)
    z_send = jnp.bitwise_and(point_voxel, ZB - 1).astype(jnp.bfloat16)
    payload = jnp.concatenate([point_feats, cotangent, xy_send[:, None], z_send[:, None]], axis=1)
    got = lax.all_to_all(payload, "group", split_axis=0, concat_axis=0, tiled=True)
    field, divisor = scatter_sums(got)
    field = field.reshape(XD, YD, 2 * ZC)
    wide = extended(field, (("space", 0), ("group", 1)), 2)
    mean_ext = wide[..., :ZC].astype(jnp.bfloat16).reshape(ER, ZC)
    gy_ext = wide[..., ZC:].reshape(ER, ZC)
    ggrid = conv_pair(mean_ext, gy_ext, banded_weights(kernel))
    parts = lax.axis_size("group")
    grads = gather_rows(ggrid, divisor, got, parts)
    back = lax.all_to_all(grads, "group", split_axis=0, concat_axis=0, tiled=True)
    return jnp.swapaxes(back, 1, 2).reshape(npts, C)


def solution(mesh):
    placed = (P(("space", "group"), None), P(("space", "group")), P(("space", "group"), None), P())
    return jax.shard_map(
        per_device,
        mesh=mesh,
        in_specs=placed,
        out_specs=P(("space", "group"), None),
        check_vma=False,
    )
```

```python
import jax
import jax.numpy as jnp
from jax import lax
from jax.experimental import pallas as pl
from jax.experimental.pallas import tpu as pltpu
from jax.sharding import PartitionSpec as P

XD = 16
YD = 16
ZB = 16
C = 32
XY = XD * YD
ZC = ZB * C
PW = 2 * C + 2
TK = 512
EX = XD + 4
EY = YD + 4
ER = EX * EY


def extended(shard, sides, width):
    for axis, dim in sides:
        size, length = (lax.axis_size(axis), shard.shape[dim])
        up = [(i, (i + 1) % size) for i in range(size - 1)]
        down = [(j, i) for i, j in up]
        last = lax.slice_in_dim(shard, length - width, length, axis=dim)
        first = lax.slice_in_dim(shard, 0, width, axis=dim)
        before = lax.ppermute(last, axis, up)
        after = lax.ppermute(first, axis, down)
        shard = jnp.concatenate([before, shard, after], axis=dim)
    return shard


def scatter_kernel(got_ref, field_ref, lo_ref, hi_ref, div_ref):
    npts = got_ref.shape[0]
    r = lax.broadcasted_iota(jnp.int32, (PW, ZC), 0)
    l = lax.broadcasted_iota(jnp.int32, (PW, ZC), 1)
    ef = (r == jnp.bitwise_and(l, C - 1)).astype(jnp.bfloat16)
    ec = (r == jnp.bitwise_and(l, C - 1) + C).astype(jnp.bfloat16)
    lane_z = (lax.broadcasted_iota(jnp.int32, (TK, ZC), 1) >> 5).astype(jnp.float32)
    lane_xy = lax.broadcasted_iota(jnp.int32, (TK, XY), 1).astype(jnp.float32)
    sf = jnp.zeros((XY, ZC), jnp.float32)
    sc = jnp.zeros((XY, ZC), jnp.float32)
    sn = jnp.zeros((XY, ZC), jnp.float32)
    over_points = (((0,), (0,)), ((), ()))
    for k in range(npts // TK):
        g = got_ref[pl.ds(k * TK, TK), :]
        wide = g.astype(jnp.float32)
        mask = lane_z == wide[:, 2 * C + 1 : 2 * C + 2]
        hot = (lane_xy == wide[:, 2 * C : 2 * C + 1]).astype(jnp.bfloat16)
        tf = jnp.dot(g, ef, preferred_element_type=jnp.float32)
        tc = jnp.dot(g, ec, preferred_element_type=jnp.float32)
        qf = jnp.where(mask, tf, 0.0).astype(jnp.bfloat16)
        qc = jnp.where(mask, tc, 0.0).astype(jnp.bfloat16)
        qn = mask.astype(jnp.bfloat16)
        sf = sf + lax.dot_general(hot, qf, over_points, preferred_element_type=jnp.float32)
        sc = sc + lax.dot_general(hot, qc, over_points, preferred_element_type=jnp.float32)
        sn = sn + lax.dot_general(hot, qn, over_points, preferred_element_type=jnp.float32)
    div = jnp.maximum(sn, 1.0)
    mean = (sf / div).astype(jnp.bfloat16).astype(jnp.float32)
    field_ref[:, :ZC] = mean
    field_ref[:, ZC:] = sc
    face = lo_ref.shape[0]
    lo_ref[:, :ZC] = mean[:face]
    lo_ref[:, ZC:] = sc[:face]
    hi_ref[:, :ZC] = mean[XY - face :]
    hi_ref[:, ZC:] = sc[XY - face :]
    div_ref[...] = div


def scatter_sums(got):
    npts = got.shape[0]
    return pl.pallas_call(
        scatter_kernel,
        out_shape=(
            jax.ShapeDtypeStruct((XY, 2 * ZC), jnp.float32),
            jax.ShapeDtypeStruct((2 * YD, 2 * ZC), jnp.float32),
            jax.ShapeDtypeStruct((2 * YD, 2 * ZC), jnp.float32),
            jax.ShapeDtypeStruct((XY, ZC), jnp.float32),
        ),
        cost_estimate=pl.CostEstimate(
            flops=2 * XY * npts * ZC * 3 + 4 * npts * PW * ZC, transcendentals=0,
            bytes_accessed=npts * PW * 2 + 3 * XY * ZC * 4,
        ),
    )(got)


def conv_kernel(m_ref, g_ref, w_ref, o_ref):
    mean = m_ref[...]
    acc = jnp.zeros((ER, ZC), jnp.float32)
    for a in range(3):
        for b in range(3):
            off = (a - 1) * EY + (b - 1)
            part = jnp.dot(mean, w_ref[a * 3 + b], preferred_element_type=jnp.float32)
            acc = acc + pltpu.roll(part, (-off) % ER, 0)
    sig = 1.0 / (1.0 + jnp.exp(-acc))
    gout = (g_ref[...] * sig * (1.0 + acc * (1.0 - sig))).astype(jnp.bfloat16)
    acc = jnp.zeros((ER, ZC), jnp.float32)
    for a in range(3):
        for b in range(3):
            off = (a - 1) * EY + (b - 1)
            part = lax.dot_general(
                gout, w_ref[8 - (a * 3 + b)], (((1,), (1,)), ((), ())), preferred_element_type=jnp.float32
            )
            acc = acc + pltpu.roll(part, (-off) % ER, 0)
    o_ref[...] = acc


def conv_pair(mean_ext, gy_ext, banded):
    return pl.pallas_call(
        conv_kernel,
        out_shape=jax.ShapeDtypeStruct((ER, ZC), jnp.float32),
        compiler_params=pltpu.CompilerParams(vmem_limit_bytes=48 * 1024 * 1024),
        cost_estimate=pl.CostEstimate(
            flops=18 * 2 * ER * ZC * ZC, transcendentals=ER * ZC,
            bytes_accessed=ER * ZC * 10 + 9 * ZC * ZC * 2,
        ),
    )(mean_ext, gy_ext, banded)


def gather_kernel(g_ref, d_ref, got_ref, o_ref, t_ref):
    npts = got_ref.shape[0]
    for x in range(XD):
        start = (x + 2) * EY + 2
        t_ref[pl.ds(x * YD, YD), :] = (g_ref[pl.ds(start, YD), :] / d_ref[pl.ds(x * YD, YD), :]).astype(t_ref.dtype)
    r = lax.broadcasted_iota(jnp.int32, (C, ZC), 0)
    l = lax.broadcasted_iota(jnp.int32, (C, ZC), 1)
    fold = (jnp.bitwise_and(l, C - 1) == r).astype(jnp.bfloat16)
    lane_z = (lax.broadcasted_iota(jnp.int32, (TK, ZC), 1) >> 5).astype(jnp.float32)
    lane_xy = lax.broadcasted_iota(jnp.int32, (TK, XY), 1).astype(jnp.float32)
    table = t_ref[...]
    block = o_ref.shape[2]
    for k in range(npts // TK):
        wide = got_ref[pl.ds(k * TK, TK), :].astype(jnp.float32)
        hot = (lane_xy == wide[:, 2 * C : 2 * C + 1]).astype(jnp.bfloat16)
        rows = jnp.dot(hot, table, preferred_element_type=jnp.float32)
        mask = lane_z == wide[:, 2 * C + 1 : 2 * C + 2]
        picked = jnp.where(mask, rows, 0.0).astype(jnp.bfloat16)
        out = lax.dot_general(fold, picked, (((1,), (1,)), ((), ())), preferred_element_type=jnp.float32)
        for j in range(TK // block):
            o_ref[k * (TK // block) + j] = out[:, j * block : (j + 1) * block].astype(o_ref.dtype)


def gather_rows(ggrid, divisor, got, parts):
    npts = got.shape[0]
    return pl.pallas_call(
        gather_kernel,
        out_shape=jax.ShapeDtypeStruct((parts, C, npts // parts), jnp.bfloat16),
        scratch_shapes=[pltpu.VMEM((XY, ZC), jnp.bfloat16)],
        cost_estimate=pl.CostEstimate(
            flops=2 * npts * XY * ZC + 2 * npts * ZC * C, transcendentals=0,
            bytes_accessed=npts * C * 2 + ER * ZC * 4 + XY * ZC * 4 + npts * PW * 2,
        ),
    )(ggrid, divisor, got)


def band_kernel(w_ref, wb_ref):
    lr = lax.broadcasted_iota(jnp.int32, (C, ZC), 0)
    lc = lax.broadcasted_iota(jnp.int32, (C, ZC), 1)
    rep_lanes = (lr == jnp.bitwise_and(lc, C - 1)).astype(jnp.bfloat16)
    lane_z = (lc >> 5).astype(jnp.float32).astype(jnp.bfloat16)
    wides = [jnp.dot(w_ref[dz], rep_lanes, preferred_element_type=jnp.float32).astype(jnp.bfloat16) for dz in range(3)]
    zero = jnp.zeros((C, ZC), jnp.bfloat16)
    for zp in range(ZB):
        block = zero
        for dz in range(3):
            block = jnp.where(lane_z == jnp.bfloat16(zp + 1 - dz), wides[dz], block)
        wb_ref[pl.ds(zp * C, C), :] = block


def banded_weights(kernel):
    taps = kernel.reshape(27, C, C)
    return pl.pallas_call(
        band_kernel,
        out_shape=jax.ShapeDtypeStruct((9, ZC, ZC), kernel.dtype),
        grid=(9,),
        in_specs=[pl.BlockSpec((3, C, C), lambda t: (t, 0, 0))],
        out_specs=pl.BlockSpec((None, ZC, ZC), lambda t: (t, 0, 0)),
        cost_estimate=pl.CostEstimate(
            flops=9 * 3 * 2 * 2 * ZC * C * ZC, transcendentals=0, bytes_accessed=9 * ZC * ZC * 2
        ),
    )(taps)


def per_device(point_feats, point_voxel, cotangent, kernel):
    npts = point_feats.shape[0]
    live = point_voxel >= 0
    xy_send = jnp.where(live, point_voxel >> 4, -1).astype(jnp.bfloat16)
    z_send = jnp.bitwise_and(point_voxel, ZB - 1).astype(jnp.bfloat16)
    payload = jnp.concatenate([point_feats, cotangent, xy_send[:, None], z_send[:, None]], axis=1)
    got = lax.all_to_all(payload, "group", split_axis=0, concat_axis=0, tiled=True)
    field, lo, hi, divisor = scatter_sums(got)
    field = field.reshape(XD, YD, 2 * ZC)
    size = lax.axis_size("space")
    up = [(i, i + 1) for i in range(size - 1)]
    down = [(j, i) for i, j in up]
    before = lax.ppermute(hi.reshape(2, YD, 2 * ZC), "space", up)
    after = lax.ppermute(lo.reshape(2, YD, 2 * ZC), "space", down)
    wide = extended(jnp.concatenate([before, field, after], axis=0), (("group", 1),), 2)
    mean_ext = wide[..., :ZC].astype(jnp.bfloat16).reshape(ER, ZC)
    gy_ext = wide[..., ZC:].reshape(ER, ZC)
    ggrid = conv_pair(mean_ext, gy_ext, banded_weights(kernel))
    parts = lax.axis_size("group")
    grads = gather_rows(ggrid, divisor, got, parts)
    back = lax.all_to_all(grads, "group", split_axis=0, concat_axis=0, tiled=True)
    return jnp.swapaxes(back, 1, 2).reshape(npts, C)


def solution(mesh):
    placed = (P(("space", "group"), None), P(("space", "group")), P(("space", "group"), None), P())
    return jax.shard_map(
        per_device,
        mesh=mesh,
        in_specs=placed,
        out_specs=P(("space", "group"), None),
        check_vma=False,
    )
```

```python
import jax
import jax.numpy as jnp
from jax import lax
from jax.experimental import pallas as pl
from jax.experimental.pallas import tpu as pltpu
from jax.sharding import PartitionSpec as P

XD = 16
YD = 16
ZB = 16
C = 32
XY = XD * YD
ZC = ZB * C
PW = 2 * C + 2
TK = 512
EX = XD + 4
EY = YD + 4
ER = EX * EY
W0, W1 = 16, 384


def extended(shard, sides, width):
    for axis, dim in sides:
        size, length = (lax.axis_size(axis), shard.shape[dim])
        up = [(i, (i + 1) % size) for i in range(size - 1)]
        down = [(j, i) for i, j in up]
        last = lax.slice_in_dim(shard, length - width, length, axis=dim)
        first = lax.slice_in_dim(shard, 0, width, axis=dim)
        before = lax.ppermute(last, axis, up)
        after = lax.ppermute(first, axis, down)
        shard = jnp.concatenate([before, shard, after], axis=dim)
    return shard


def scatter_kernel(got_ref, field_ref, lo_ref, hi_ref, div_ref):
    npts = got_ref.shape[0]
    r = lax.broadcasted_iota(jnp.int32, (PW, ZC), 0)
    l = lax.broadcasted_iota(jnp.int32, (PW, ZC), 1)
    ef = (r == jnp.bitwise_and(l, C - 1)).astype(jnp.bfloat16)
    ec = (r == jnp.bitwise_and(l, C - 1) + C).astype(jnp.bfloat16)
    lane_z = (lax.broadcasted_iota(jnp.int32, (TK, ZC), 1) >> 5).astype(jnp.float32)
    lane_xy = lax.broadcasted_iota(jnp.int32, (TK, XY), 1).astype(jnp.float32)
    sf = jnp.zeros((XY, ZC), jnp.float32)
    sc = jnp.zeros((XY, ZC), jnp.float32)
    sn = jnp.zeros((XY, ZC), jnp.float32)
    over_points = (((0,), (0,)), ((), ()))
    for k in range(npts // TK):
        g = got_ref[pl.ds(k * TK, TK), :]
        wide = g.astype(jnp.float32)
        mask = lane_z == wide[:, 2 * C + 1 : 2 * C + 2]
        hot = (lane_xy == wide[:, 2 * C : 2 * C + 1]).astype(jnp.bfloat16)
        tf = jnp.dot(g, ef, preferred_element_type=jnp.float32)
        tc = jnp.dot(g, ec, preferred_element_type=jnp.float32)
        qf = jnp.where(mask, tf, 0.0).astype(jnp.bfloat16)
        qc = jnp.where(mask, tc, 0.0).astype(jnp.bfloat16)
        qn = mask.astype(jnp.bfloat16)
        sf = sf + lax.dot_general(hot, qf, over_points, preferred_element_type=jnp.float32)
        sc = sc + lax.dot_general(hot, qc, over_points, preferred_element_type=jnp.float32)
        sn = sn + lax.dot_general(hot, qn, over_points, preferred_element_type=jnp.float32)
    div = jnp.maximum(sn, 1.0)
    mean = (sf / div).astype(jnp.bfloat16).astype(jnp.float32)
    field_ref[:, :ZC] = mean
    field_ref[:, ZC:] = sc
    face = lo_ref.shape[0]
    lo_ref[:, :ZC] = mean[:face]
    lo_ref[:, ZC:] = sc[:face]
    hi_ref[:, :ZC] = mean[XY - face :]
    hi_ref[:, ZC:] = sc[XY - face :]
    div_ref[...] = div


def scatter_sums(got):
    npts = got.shape[0]
    return pl.pallas_call(
        scatter_kernel,
        out_shape=(
            jax.ShapeDtypeStruct((XY, 2 * ZC), jnp.float32),
            jax.ShapeDtypeStruct((2 * YD, 2 * ZC), jnp.float32),
            jax.ShapeDtypeStruct((2 * YD, 2 * ZC), jnp.float32),
            jax.ShapeDtypeStruct((XY, ZC), jnp.float32),
        ),
        cost_estimate=pl.CostEstimate(
            flops=2 * XY * npts * ZC * 3 + 4 * npts * PW * ZC, transcendentals=0,
            bytes_accessed=npts * PW * 2 + 3 * XY * ZC * 4,
        ),
    )(got)


def conv_kernel(m_ref, g_ref, w_ref, o_ref):
    mean = m_ref[...]
    acc = jnp.zeros((ER, ZC), jnp.float32)
    for a in range(3):
        for b in range(3):
            off = (a - 1) * EY + (b - 1)
            part = jnp.dot(mean, w_ref[a * 3 + b], preferred_element_type=jnp.float32)
            acc = acc + pltpu.roll(part, (-off) % ER, 0)
    sig = 1.0 / (1.0 + jnp.exp(-acc))
    gout = (g_ref[...] * sig * (1.0 + acc * (1.0 - sig))).astype(jnp.bfloat16)[W0:W1]
    acc = jnp.zeros((W1 - W0, ZC), jnp.float32)
    for a in range(3):
        for b in range(3):
            off = (a - 1) * EY + (b - 1)
            part = lax.dot_general(
                gout, w_ref[8 - (a * 3 + b)], (((1,), (1,)), ((), ())), preferred_element_type=jnp.float32
            )
            acc = acc + pltpu.roll(part, (-off) % (W1 - W0), 0)
    o_ref[pl.ds(W0, W1 - W0), :] = acc


def conv_pair(mean_ext, gy_ext, banded):
    return pl.pallas_call(
        conv_kernel,
        out_shape=jax.ShapeDtypeStruct((ER, ZC), jnp.float32),
        compiler_params=pltpu.CompilerParams(vmem_limit_bytes=48 * 1024 * 1024),
        cost_estimate=pl.CostEstimate(
            flops=18 * 2 * ER * ZC * ZC, transcendentals=ER * ZC,
            bytes_accessed=ER * ZC * 10 + 9 * ZC * ZC * 2,
        ),
    )(mean_ext, gy_ext, banded)


def gather_kernel(g_ref, d_ref, got_ref, o_ref, t_ref):
    npts = got_ref.shape[0]
    for x in range(XD):
        start = (x + 2) * EY + 2
        t_ref[pl.ds(x * YD, YD), :] = (g_ref[pl.ds(start, YD), :] / d_ref[pl.ds(x * YD, YD), :]).astype(t_ref.dtype)
    r = lax.broadcasted_iota(jnp.int32, (C, ZC), 0)
    l = lax.broadcasted_iota(jnp.int32, (C, ZC), 1)
    fold = (jnp.bitwise_and(l, C - 1) == r).astype(jnp.bfloat16)
    lane_z = (lax.broadcasted_iota(jnp.int32, (TK, ZC), 1) >> 5).astype(jnp.float32)
    lane_xy = lax.broadcasted_iota(jnp.int32, (TK, XY), 1).astype(jnp.float32)
    table = t_ref[...]
    block = o_ref.shape[2]
    for k in range(npts // TK):
        wide = got_ref[pl.ds(k * TK, TK), :].astype(jnp.float32)
        hot = (lane_xy == wide[:, 2 * C : 2 * C + 1]).astype(jnp.bfloat16)
        rows = jnp.dot(hot, table, preferred_element_type=jnp.float32)
        mask = lane_z == wide[:, 2 * C + 1 : 2 * C + 2]
        picked = jnp.where(mask, rows, 0.0).astype(jnp.bfloat16)
        out = lax.dot_general(fold, picked, (((1,), (1,)), ((), ())), preferred_element_type=jnp.float32)
        for j in range(TK // block):
            o_ref[k * (TK // block) + j] = out[:, j * block : (j + 1) * block].astype(o_ref.dtype)


def gather_rows(ggrid, divisor, got, parts):
    npts = got.shape[0]
    return pl.pallas_call(
        gather_kernel,
        out_shape=jax.ShapeDtypeStruct((parts, C, npts // parts), jnp.bfloat16),
        scratch_shapes=[pltpu.VMEM((XY, ZC), jnp.bfloat16)],
        cost_estimate=pl.CostEstimate(
            flops=2 * npts * XY * ZC + 2 * npts * ZC * C, transcendentals=0,
            bytes_accessed=npts * C * 2 + ER * ZC * 4 + XY * ZC * 4 + npts * PW * 2,
        ),
    )(ggrid, divisor, got)


def band_kernel(w_ref, wb_ref):
    lr = lax.broadcasted_iota(jnp.int32, (C, ZC), 0)
    lc = lax.broadcasted_iota(jnp.int32, (C, ZC), 1)
    rep_lanes = (lr == jnp.bitwise_and(lc, C - 1)).astype(jnp.bfloat16)
    lane_z = (lc >> 5).astype(jnp.float32).astype(jnp.bfloat16)
    wides = [jnp.dot(w_ref[dz], rep_lanes, preferred_element_type=jnp.float32).astype(jnp.bfloat16) for dz in range(3)]
    zero = jnp.zeros((C, ZC), jnp.bfloat16)
    for zp in range(ZB):
        block = zero
        for dz in range(3):
            block = jnp.where(lane_z == jnp.bfloat16(zp + 1 - dz), wides[dz], block)
        wb_ref[pl.ds(zp * C, C), :] = block


def banded_weights(kernel):
    taps = kernel.reshape(27, C, C)
    return pl.pallas_call(
        band_kernel,
        out_shape=jax.ShapeDtypeStruct((9, ZC, ZC), kernel.dtype),
        grid=(9,),
        in_specs=[pl.BlockSpec((3, C, C), lambda t: (t, 0, 0))],
        out_specs=pl.BlockSpec((None, ZC, ZC), lambda t: (t, 0, 0)),
        cost_estimate=pl.CostEstimate(
            flops=9 * 3 * 2 * 2 * ZC * C * ZC, transcendentals=0, bytes_accessed=9 * ZC * ZC * 2
        ),
    )(taps)


def per_device(point_feats, point_voxel, cotangent, kernel):
    npts = point_feats.shape[0]
    live = point_voxel >= 0
    xy_send = jnp.where(live, point_voxel >> 4, -1).astype(jnp.bfloat16)
    z_send = jnp.bitwise_and(point_voxel, ZB - 1).astype(jnp.bfloat16)
    payload = jnp.concatenate([point_feats, cotangent, xy_send[:, None], z_send[:, None]], axis=1)
    got = lax.all_to_all(payload, "group", split_axis=0, concat_axis=0, tiled=True)
    field, lo, hi, divisor = scatter_sums(got)
    field = field.reshape(XD, YD, 2 * ZC)
    size = lax.axis_size("space")
    up = [(i, i + 1) for i in range(size - 1)]
    down = [(j, i) for i, j in up]
    before = lax.ppermute(hi.reshape(2, YD, 2 * ZC), "space", up)
    after = lax.ppermute(lo.reshape(2, YD, 2 * ZC), "space", down)
    wide = extended(jnp.concatenate([before, field, after], axis=0), (("group", 1),), 2)
    mean_ext = wide[..., :ZC].astype(jnp.bfloat16).reshape(ER, ZC)
    gy_ext = wide[..., ZC:].reshape(ER, ZC)
    ggrid = conv_pair(mean_ext, gy_ext, banded_weights(kernel))
    parts = lax.axis_size("group")
    grads = gather_rows(ggrid, divisor, got, parts)
    back = lax.all_to_all(grads, "group", split_axis=0, concat_axis=0, tiled=True)
    return jnp.swapaxes(back, 1, 2).reshape(npts, C)


def solution(mesh):
    placed = (P(("space", "group"), None), P(("space", "group")), P(("space", "group"), None), P())
    return jax.shard_map(
        per_device,
        mesh=mesh,
        in_specs=placed,
        out_specs=P(("space", "group"), None),
        check_vma=False,
    )
```
